256 devices in a mesh: scen: 64 (over y, x, z_hi), rootr: 2 (over core), rootc: 2 (over z_lo).
Axes of the slice: x: 4, y: 4, z: 8 (z_hi: 4, z_lo: 2; z = z_hi * 2 + z_lo), core: 2. Of those that a mesh axis runs over, the one named last changes fastest.
Arguments:
- start_guess: float32 [8192, 256], P(('scen', 'rootr'), 'rootc'), may hold values from -6 to 6
- right_side: float32 [8192, 256], P(('scen', 'rootr'), 'rootc'), may hold values from -6 to 6
- root_diagonal: float32 [8192], P(('scen', 'rootr')), may hold values from 1 to 4
- preconditioner: bfloat16 [8192, 8192], P(('scen', 'rootr')), may hold values from -0.015625 to 0.015625
- border_block: bfloat16 [128, 512, 768], P(('scen', 'rootr'), 'rootc'), may hold values from -0.21875 to 0.21875
- coupling_inverse: bfloat16 [128, 512, 512], P(('scen', 'rootr'), 'rootc'), may hold values from -0.25 to 0.25
- border_count: int32 [128], P(('scen', 'rootr')), may hold values from 64 to 512, as said below
- column_tiles: int32 [128, 6], P(('scen', 'rootr')), may hold values from 0 to 63, as said below
Outputs:
- final_iterate: float32 [8192, 256], P(('scen', 'rootr'), 'rootc')
The draws below stay inside these ranges and needn't reach their ends.
Inputs may be any that keep to these rules, and one draw needn't show every extreme that they name: A scenario's live border rows are its first border_count rows; some scenario has exactly 512. `column_tiles`: each row names 6 different tiles in rising order.
All inputs are finite; a program needn't handle non-finite values.
Results may differ from the reference program's by a relative error of at most 0.0022.
Values may be sent and summed in bfloat16 or wider, within the bound.
No kernel may reach another device: no remote copies, remote signals or barrier semaphores. Data moves between devices by JAX's collectives and lax.ppermute only.
A program may use at most 64 MiB of HBM per device.

```python
import math
import jax
import jax.numpy as jnp
from jax import lax

ORDER = 8192
RHS = 256
BORDER = 512
TILE = 128
TOUCHED = 6
ITERS = 1
SCEN = 128
NTILES = 64
COUPLED = 768


def draw_border_count(key, part):
    first_key, second_key = jax.random.split(key)
    divisor = jax.random.randint(first_key, (SCEN,), 1, 9)
    counts = BORDER // divisor
    chosen = jax.random.randint(second_key, (), 0, SCEN)
    return jnp.where(jnp.arange(SCEN) == chosen, BORDER, counts).astype(jnp.int32)


def draw_column_tiles(key, part):
    scores = jax.random.randint(key, (SCEN, NTILES), 0, 1 << 20) * NTILES + jnp.arange(NTILES)[None, :]
    ordering = jnp.argsort(scores, axis=1)[:, :TOUCHED]
    return jnp.sort(ordering, axis=1).astype(jnp.int32)


def shard_levels(key, extent, pieces, least, largest):
    loudness, own = 1.0, jax.random.fold_in(key, 6)
    for position, parts in pieces:
        draws = jnp.exp(jax.random.uniform(jax.random.fold_in(own, position), (parts,), jnp.float32, least / len(pieces), largest / len(pieces)))
        loudness = loudness * jnp.repeat(draws, extent[position] // parts).reshape([-1 if axis == position else 1 for axis in range(len(extent))])
    return loudness


def centred(rng, extent, width, most, pieces=(), dtype=jnp.bfloat16):
    loudness = shard_levels(rng, extent, pieces, -0.22, 0.18) if pieces else 1.0
    values = jax.random.normal(rng, extent, jnp.float32) * width * loudness
    return jnp.minimum(jnp.maximum(values, -most), most).astype(dtype)


def setup_inputs(seed: int = 0) -> dict:
    seeds = jax.random.split(jax.random.key(seed), 9)
    start_guess = centred(seeds[0], (ORDER, RHS), 1.0, 6.0, ((0, 128), (1, 2)), jnp.float32)
    right_side = centred(seeds[1], (ORDER, RHS), 1.0, 6.0, ((0, 128), (1, 2)), jnp.float32)
    root_diagonal = jnp.clip(jnp.exp(math.log(4.0) - 1.3862944 * jax.random.uniform(seeds[2], (ORDER,), jnp.float32) ** shard_levels(seeds[2], (ORDER,), ((0, 128),), -0.2, 0.2)), 1.0, 4.0)
    preconditioner = centred(seeds[3], (ORDER, ORDER), (16 * ORDER) ** -0.5, 0.015625, ((0, 128),))
    border_block = centred(seeds[4], (SCEN, BORDER, COUPLED), COUPLED ** -0.5, 0.21875, ((0, 128), (1, 2)))
    coupling_inverse = centred(seeds[5], (SCEN, BORDER, BORDER), BORDER ** -0.5, 0.25, ((0, 128), (1, 2)))
    border_count = draw_border_count(jax.random.fold_in(seeds[8], 71), 0)
    column_tiles = draw_column_tiles(jax.random.fold_in(seeds[8], 71), 0)
    return {"start_guess": start_guess, "right_side": right_side, "root_diagonal": root_diagonal, "preconditioner": preconditioner, "border_block": border_block, "coupling_inverse": coupling_inverse, "border_count": border_count, "column_tiles": column_tiles}


def scenario_term(iterate_low, border, inverse_rows, live_count, tile_ids):
    picked = iterate_low.reshape(NTILES, TILE, RHS)[tile_ids].reshape(COUPLED, RHS)
    live_rows = (jnp.arange(BORDER) < live_count)[:, None]
    border_values = jnp.dot(border, picked, preferred_element_type=jnp.float32)
    border_values = jnp.where(live_rows, border_values, 0.0).astype(jnp.bfloat16)
    solved = jnp.dot(inverse_rows, border_values, preferred_element_type=jnp.float32)
    solved = jnp.where(live_rows, solved, 0.0).astype(jnp.bfloat16)
    return jnp.dot(border.T, solved, preferred_element_type=jnp.float32)


def reference(start_guess, right_side, root_diagonal, preconditioner, border_block, coupling_inverse, border_count, column_tiles):
    iterate = start_guess
    for iteration in range(ITERS):
        iterate_low = iterate.astype(jnp.bfloat16)

        def accumulate(running, scenario):
            border, inverse_rows, live_count, tile_ids = scenario
            term = scenario_term(iterate_low, border, inverse_rows, live_count, tile_ids)
            running = running.reshape(NTILES, TILE, RHS).at[tile_ids].add(term.reshape(TOUCHED, TILE, RHS))
            return running.reshape(ORDER, RHS), None

        coupling, unused = lax.scan(accumulate, jnp.zeros((ORDER, RHS), jnp.float32), (border_block, coupling_inverse, border_count, column_tiles))
        residual = right_side - root_diagonal[:, None] * iterate + coupling
        iterate = iterate + jnp.dot(preconditioner, residual.astype(jnp.bfloat16), preferred_element_type=jnp.float32)
    return iterate
```

```python
import functools

import jax
import jax.numpy as jnp
from jax import lax
from jax.experimental import pallas as pl
from jax.experimental.pallas import tpu as pltpu
from jax.sharding import Mesh
from jax.sharding import PartitionSpec as P

TILE = 128
HALF = 64
RING = 4
Y, X, Z, CORE, SIDE = "scen_0", "scen_1", "scen_2", "rootr", "rootc"
SCEN_ROOTR = (Y, X, Z, CORE)
SWAP = [(0, 1), (1, 0)]
F32 = jnp.float32
BF16 = jnp.bfloat16

VMEM = pl.BlockSpec(memory_space=pltpu.VMEM)
SMEM = pl.BlockSpec(memory_space=pltpu.SMEM)


def swap(value, axis):
    return lax.ppermute(value, axis, SWAP)


def from_ahead(value, axis, distance):
    return lax.ppermute(value, axis, [(i, (i - distance) % RING) for i in range(RING)])


def to_ahead(value, axis, distance):
    return lax.ppermute(value, axis, [(i, (i + distance) % RING) for i in range(RING)])


def ring_pieces(value, axis):
    return [value] + [from_ahead(value, axis, k) for k in range(1, RING)]


def ring_gather(value):
    line = jnp.stack(ring_pieces(value, Z))
    plane = jnp.concatenate(ring_pieces(line, X))
    return ring_pieces(plane, Y)


def place(tile, where):
    dy = (tile // 16 - where[0]) % RING
    dx = ((tile // 4) % 4 - where[1]) % RING
    dz = (tile % 4 - where[2]) % RING
    return dy, dx * 4 + dz


def pick_kernel(where, own_ids, other_ids, p0, p1, p2, p3, own_ref, other_ref):
    pieces = (p0, p1, p2, p3)
    for ids, out in ((other_ids, other_ref), (own_ids, own_ref)):
        for j in range(ids.shape[1]):
            dy, rest = place(ids[0, j], where)
            for k, piece in enumerate(pieces):

                @pl.when(dy == k)
                def _():
                    out[j] = piece[rest]


def scenario_kernel(
    where, count, own_picked, other_picked, border_own, border_other, inverse_own, inverse_other,
    keep_ref, send_ref, picked, values,
):
    core, side = where[3], where[4]
    half_rows = border_own.shape[0]
    tiles = own_picked.shape[0]
    for j in range(tiles):
        picked[pl.ds(pl.multiple_of(j * TILE + core * HALF, HALF), HALF), :] = own_picked[j]
        picked[pl.ds(pl.multiple_of(j * TILE + (1 - core) * HALF, HALF), HALF), :] = other_picked[j]
    rows = lax.broadcasted_iota(jnp.int32, (half_rows, values.shape[1]), 0)
    own_start = pl.multiple_of(side * half_rows, half_rows)
    other_start = pl.multiple_of((1 - side) * half_rows, half_rows)
    live = count[0]

    def masked(product, start):
        return jnp.where(rows + start < live, product, 0.0).astype(BF16)

    whole = picked[...]
    values[pl.ds(own_start, half_rows), :] = masked(
        jnp.dot(border_own[...], whole, preferred_element_type=F32), own_start
    )
    values[pl.ds(other_start, half_rows), :] = masked(
        jnp.dot(border_other[...], whole, preferred_element_type=F32), other_start
    )
    operand = values[...]
    solved_own = masked(jnp.dot(inverse_own[...], operand, preferred_element_type=F32), own_start)
    solved_other = masked(jnp.dot(inverse_other[...], operand, preferred_element_type=F32), other_start)
    numbers = (((0,), (0,)), ((), ()))
    term = lax.dot_general(border_own[...], solved_own, numbers, preferred_element_type=F32)
    term += lax.dot_general(border_other[...], solved_other, numbers, preferred_element_type=F32)
    term = term.reshape(tiles, 2, HALF, term.shape[1])

    @pl.when(core == 0)
    def _():
        keep_ref[...] = term[:, 0]
        send_ref[...] = term[:, 1]

    @pl.when(core == 1)
    def _():
        keep_ref[...] = term[:, 1]
        send_ref[...] = term[:, 0]


def scatter_kernel(where, own_ids, other_ids, keep, arrived, near, c1, c2, c3, total):
    total[...] = jnp.zeros_like(total)
    for ids, terms in ((own_ids, keep), (other_ids, arrived)):
        for j in range(ids.shape[1]):
            dy, rest = place(ids[0, j], where)
            total[dy * 16 + rest] += terms[j]
    near[...] = total[0:16]
    for k, chunk in enumerate((c1, c2, c3)):
        chunk[...] = total[16 * (k + 1) : 16 * (k + 2)].astype(BF16)


def update_kernel(where, start, precond, *refs):
    pieces, (out_ref, whole) = refs[:8], refs[8:]
    y, x, z, core = where[0], where[1], where[2], where[3]
    for side in range(2):
        half = core if side == 0 else 1 - core
        for k in range(RING):
            piece = pieces[side * RING + k]
            base_y = ((y + k) % RING) * 16
            for i in range(RING):
                base_x = base_y + ((x + i) % RING) * 4
                for j in range(RING):
                    tile = base_x + (z + j) % RING
                    at = pl.multiple_of(tile * TILE + half * HALF, HALF)
                    whole[pl.ds(at, HALF), :] = piece[i * RING + j]
    out_ref[...] = start[...] + jnp.dot(precond[...], whole[...], preferred_element_type=F32)


def call(kernel, specs, outs, scratch=(), flops=0, moved=0):
    return pl.pallas_call(
        kernel,
        out_shape=outs,
        in_specs=specs,
        out_specs=jax.tree.map(lambda _: VMEM, outs),
        scratch_shapes=scratch,
        cost_estimate=pl.CostEstimate(flops=flops, bytes_accessed=moved, transcendentals=0),
        compiler_params=pltpu.CompilerParams(vmem_limit_bytes=32 * 1024 * 1024),
    )


def local(
    start_guess,
    right_side,
    root_diagonal,
    preconditioner,
    border_block,
    coupling_inverse,
    border_count,
    column_tiles,
):
    rows, cols = start_guess.shape
    shape = jax.ShapeDtypeStruct
    where = jnp.stack([lax.axis_index(a) for a in (Y, X, Z, CORE, SIDE)]).astype(jnp.int32)
    border, inverse = border_block[0], coupling_inverse[0]
    tiles = column_tiles.shape[1]

    pieces = ring_gather(start_guess.astype(BF16))
    other_tiles = swap(column_tiles, CORE)
    border_other = swap(border, SIDE)
    inverse_other = swap(inverse, SIDE)

    own_half, for_other = call(
        pick_kernel,
        [SMEM] * 3 + [VMEM] * 4,
        [shape((tiles, HALF, cols), BF16)] * 2,
    )(where, column_tiles, other_tiles, *pieces)
    other_half = swap(for_other, CORE)
    keep, send = call(
        scenario_kernel,
        [SMEM] * 2 + [VMEM] * 6,
        [shape((tiles, HALF, cols), F32)] * 2,
        [pltpu.VMEM((tiles * TILE, cols), BF16), pltpu.VMEM((2 * border.shape[0], cols), BF16)],
    )(where, border_count, own_half, other_half, border, border_other, inverse, inverse_other)
    arrived = swap(send, CORE)
    chunk = (16, HALF, cols)
    near, c1, c2, c3 = call(
        scatter_kernel,
        [SMEM] * 3 + [VMEM] * 2,
        [shape(chunk, F32)] + [shape(chunk, BF16)] * 3,
        [pltpu.VMEM((64, HALF, cols), F32)],
    )(where, column_tiles, other_tiles, keep, arrived)

    plane = near
    for k, c in enumerate((c1, c2, c3)):
        plane = plane + to_ahead(c, Y, k + 1).astype(F32)
    plane = plane.reshape(RING, RING, HALF, cols)
    line = plane[0]
    for k in range(1, RING):
        line = line + to_ahead(plane[k].astype(BF16), X, k).astype(F32)
    total = line[0]
    for k in range(1, RING):
        total = total + to_ahead(line[k].astype(BF16), Z, k).astype(F32)
    residual = right_side - root_diagonal[:, None] * start_guess + total

    mine = ring_gather(residual.astype(BF16))
    partners = [swap(piece, CORE) for piece in mine]
    return call(
        update_kernel,
        [SMEM] + [VMEM] * 10,
        shape((rows, cols), F32),
        [pltpu.VMEM((preconditioner.shape[1], cols), BF16)],
    )(where, start_guess, preconditioner, *mine, *partners)


def solution(mesh):
    torus = Mesh(
        mesh.devices.reshape(RING, RING, RING, mesh.shape["rootr"], mesh.shape["rootc"]),
        (Y, X, Z, CORE, SIDE),
    )
    in_specs = (
        P(SCEN_ROOTR, SIDE),
        P(SCEN_ROOTR, SIDE),
        P(SCEN_ROOTR),
        P(SCEN_ROOTR, None),
        P(SCEN_ROOTR, SIDE, None),
        P(SCEN_ROOTR, SIDE, None),
        P(SCEN_ROOTR),
        P(SCEN_ROOTR, None),
    )
    return jax.shard_map(
        local, mesh=torus, in_specs=in_specs, out_specs=P(SCEN_ROOTR, SIDE), check_vma=False
    )
```

```python
import functools

import jax
import jax.numpy as jnp
from jax import lax
from jax.experimental import pallas as pl
from jax.experimental.pallas import tpu as pltpu
from jax.sharding import Mesh
from jax.sharding import PartitionSpec as P

TILE = 128
HALF = 64
RING = 4
Y, X, Z, CORE, SIDE = "scen_0", "scen_1", "scen_2", "rootr", "rootc"
SCEN_ROOTR = (Y, X, Z, CORE)
SWAP = [(0, 1), (1, 0)]
F32 = jnp.float32
BF16 = jnp.bfloat16

VMEM = pl.BlockSpec(memory_space=pltpu.VMEM)
SMEM = pl.BlockSpec(memory_space=pltpu.SMEM)


def swap(value, axis):
    return lax.ppermute(value, axis, SWAP)


def from_ahead(value, axis, distance):
    return lax.ppermute(value, axis, [(i, (i - distance) % RING) for i in range(RING)])


def to_ahead(value, axis, distance):
    return lax.ppermute(value, axis, [(i, (i + distance) % RING) for i in range(RING)])


def ring_pieces(value, axis):
    return [value] + [from_ahead(value, axis, k) for k in range(1, RING)]


def pair(axis, value, first):
    other = [1, 0, 3, 2] if first else [3, 2, 1, 0]
    return lax.ppermute(value, axis, list(enumerate(other)))


def line_gather(value):
    two = jnp.stack([value, pair(Z, value, True)])
    return jnp.concatenate([two, pair(Z, two, False)])


def line_slot(tile_z, z):
    return jnp.where(
        tile_z == z, 0, jnp.where(tile_z == (z ^ 1), 1, jnp.where(tile_z == 3 - z, 2, 3))
    )


def place(tile, where):
    dy = (tile // 16 - where[0]) % RING
    dx = ((tile // 4) % 4 - where[1]) % RING
    return dy, dx * 4 + line_slot(tile % 4, where[2])


def pick_kernel(where, own_ids, other_ids, p0, p1, p2, p3, own_ref, other_ref):
    pieces = (p0, p1, p2, p3)
    for ids, out in ((other_ids, other_ref), (own_ids, own_ref)):
        for j in range(ids.shape[1]):
            dy, rest = place(ids[0, j], where)
            for k, piece in enumerate(pieces):

                @pl.when(dy == k)
                def _():
                    out[j] = piece[rest]


def scenario_kernel(
    where, count, own_picked, other_picked, border_own, border_other, inverse_own, inverse_other,
    keep_ref, send_ref, picked, values,
):
    core, side = where[3], where[4]
    half_rows = border_own.shape[0]
    tiles = own_picked.shape[0]
    for j in range(tiles):
        picked[pl.ds(pl.multiple_of(j * TILE + core * HALF, HALF), HALF), :] = own_picked[j]
        picked[pl.ds(pl.multiple_of(j * TILE + (1 - core) * HALF, HALF), HALF), :] = other_picked[j]
    rows = lax.broadcasted_iota(jnp.int32, (half_rows, values.shape[1]), 0)
    own_start = pl.multiple_of(side * half_rows, half_rows)
    other_start = pl.multiple_of((1 - side) * half_rows, half_rows)
    live = count[0]

    def masked(product, start):
        return jnp.where(rows + start < live, product, 0.0).astype(BF16)

    whole = picked[...]
    values[pl.ds(own_start, half_rows), :] = masked(
        jnp.dot(border_own[...], whole, preferred_element_type=F32), own_start
    )
    values[pl.ds(other_start, half_rows), :] = masked(
        jnp.dot(border_other[...], whole, preferred_element_type=F32), other_start
    )
    operand = values[...]
    solved_own = masked(jnp.dot(inverse_own[...], operand, preferred_element_type=F32), own_start)
    solved_other = masked(jnp.dot(inverse_other[...], operand, preferred_element_type=F32), other_start)
    numbers = (((0,), (0,)), ((), ()))
    term = lax.dot_general(border_own[...], solved_own, numbers, preferred_element_type=F32)
    term += lax.dot_general(border_other[...], solved_other, numbers, preferred_element_type=F32)
    term = term.reshape(tiles, 2, HALF, term.shape[1])

    @pl.when(core == 0)
    def _():
        keep_ref[...] = term[:, 0]
        send_ref[...] = term[:, 1]

    @pl.when(core == 1)
    def _():
        keep_ref[...] = term[:, 1]
        send_ref[...] = term[:, 0]


def scatter_kernel(where, own_ids, other_ids, keep, arrived, near, c1, c2, c3, total):
    total[...] = jnp.zeros_like(total)
    for ids, terms in ((own_ids, keep), (other_ids, arrived)):
        for j in range(ids.shape[1]):
            dy, rest = place(ids[0, j], where)
            total[dy * 16 + rest] += terms[j]
    near[...] = total[0:16]
    for k, chunk in enumerate((c1, c2, c3)):
        chunk[...] = total[16 * (k + 1) : 16 * (k + 2)].astype(BF16)


def update_kernel(where, start, precond, b1, b2, b3, *refs):
    pieces, (o0, o1, o2, o3, whole) = refs[:8], refs[8:]
    y, x, z, core = where[0], where[1], where[2], where[3]
    slots = (z, z ^ 1, 3 - z, (3 - z) ^ 1)
    for side in range(2):
        half = core if side == 0 else 1 - core
        for i in range(RING):
            piece = pieces[side * RING + i]
            base = ((x + i) % RING) * 4
            for j in range(RING):
                at = pl.multiple_of((base + slots[j]) * TILE + half * HALF, HALF)
                whole[pl.ds(at, HALF), :] = piece[j]
    operand = whole[...]
    span = operand.shape[0]
    own = precond[:, pl.ds(pl.multiple_of(y * span, span), span)]
    o0[...] = start[...] + jnp.dot(own, operand, preferred_element_type=F32)
    for block, out in ((b1, o1), (b2, o2), (b3, o3)):
        out[...] = jnp.dot(block[...], operand, preferred_element_type=F32)


def call(kernel, specs, outs, scratch=(), flops=0, moved=0):
    return pl.pallas_call(
        kernel,
        out_shape=outs,
        in_specs=specs,
        out_specs=jax.tree.map(lambda _: VMEM, outs),
        scratch_shapes=scratch,
        cost_estimate=pl.CostEstimate(flops=flops, bytes_accessed=moved, transcendentals=0),
        compiler_params=pltpu.CompilerParams(vmem_limit_bytes=32 * 1024 * 1024),
    )


def local(
    start_guess,
    right_side,
    root_diagonal,
    preconditioner,
    border_block,
    coupling_inverse,
    border_count,
    column_tiles,
):
    rows, cols = start_guess.shape
    shape = jax.ShapeDtypeStruct
    where = jnp.stack([lax.axis_index(a) for a in (Y, X, Z, CORE, SIDE)]).astype(jnp.int32)
    border, inverse = border_block[0], coupling_inverse[0]
    tiles = column_tiles.shape[1]

    line = line_gather(start_guess.astype(BF16))
    plane = jnp.concatenate(ring_pieces(line, X))
    pieces = ring_pieces(plane, Y)
    span = preconditioner.shape[1] // RING
    blocks = []
    for k in range(1, RING):
        first = ((where[0] + k) % RING) * span
        columns = lax.dynamic_slice_in_dim(preconditioner, first, span, 1)
        blocks.append(to_ahead(columns, Y, k))
    other_tiles = swap(column_tiles, CORE)
    border_other = swap(border, SIDE)
    inverse_other = swap(inverse, SIDE)

    own_half, for_other = call(
        pick_kernel,
        [SMEM] * 3 + [VMEM] * 4,
        [shape((tiles, HALF, cols), BF16)] * 2,
    )(where, column_tiles, other_tiles, *pieces)
    other_half = swap(for_other, CORE)
    keep, send = call(
        scenario_kernel,
        [SMEM] * 2 + [VMEM] * 6,
        [shape((tiles, HALF, cols), F32)] * 2,
        [pltpu.VMEM((tiles * TILE, cols), BF16), pltpu.VMEM((2 * border.shape[0], cols), BF16)],
    )(where, border_count, own_half, other_half, border, border_other, inverse, inverse_other)
    arrived = swap(send, CORE)
    chunk = (16, HALF, cols)
    near, c1, c2, c3 = call(
        scatter_kernel,
        [SMEM] * 3 + [VMEM] * 2,
        [shape(chunk, F32)] + [shape(chunk, BF16)] * 3,
        [pltpu.VMEM((64, HALF, cols), F32)],
    )(where, column_tiles, other_tiles, keep, arrived)

    plane = near
    for k, c in enumerate((c1, c2, c3)):
        plane = plane + to_ahead(c, Y, k + 1).astype(F32)
    plane = plane.reshape(RING, RING, HALF, cols)
    line = plane[0]
    for k in range(1, RING):
        line = line + to_ahead(plane[k].astype(BF16), X, k).astype(F32)
    own_terms = right_side - root_diagonal[:, None] * start_guess
    line = line + jnp.concatenate([own_terms[None], jnp.zeros_like(line[1:])])
    met = pair(Z, line.astype(BF16), True).astype(F32)
    line = line + jnp.stack([met[1], met[0], met[3], met[2]])
    met = pair(Z, line.astype(BF16), False).astype(F32)
    line = line + jnp.concatenate([met[2:], met[:2]])

    mine = ring_pieces(line.astype(BF16), X)
    partners = [swap(piece, CORE) for piece in mine]
    parts = call(
        update_kernel,
        [SMEM] + [VMEM] * 13,
        [shape((rows, cols), F32)] * RING,
        [pltpu.VMEM((span, cols), BF16)],
    )(where, start_guess, preconditioner, *blocks, *mine, *partners)
    out = parts[0]
    for k in range(1, RING):
        out = out + from_ahead(parts[k], Y, k)
    return out


def solution(mesh):
    torus = Mesh(
        mesh.devices.reshape(RING, RING, RING, mesh.shape["rootr"], mesh.shape["rootc"]),
        (Y, X, Z, CORE, SIDE),
    )
    in_specs = (
        P(SCEN_ROOTR, SIDE),
        P(SCEN_ROOTR, SIDE),
        P(SCEN_ROOTR),
        P(SCEN_ROOTR, None),
        P(SCEN_ROOTR, SIDE, None),
        P(SCEN_ROOTR, SIDE, None),
        P(SCEN_ROOTR),
        P(SCEN_ROOTR, None),
    )
    return jax.shard_map(
        local, mesh=torus, in_specs=in_specs, out_specs=P(SCEN_ROOTR, SIDE), check_vma=False
    )
```

```python
import functools

import jax
import jax.numpy as jnp
from jax import lax
from jax.experimental import pallas as pl
from jax.experimental.pallas import tpu as pltpu
from jax.sharding import Mesh
from jax.sharding import PartitionSpec as P

TILE = 128
HALF = 64
RING = 4
Y, X, Z, CORE, SIDE = "scen_0", "scen_1", "scen_2", "rootr", "rootc"
SCEN_ROOTR = (Y, X, Z, CORE)
SWAP = [(0, 1), (1, 0)]
F32 = jnp.float32
BF16 = jnp.bfloat16

VMEM = pl.BlockSpec(memory_space=pltpu.VMEM)
SMEM = pl.BlockSpec(memory_space=pltpu.SMEM)


def swap(value, axis):
    return lax.ppermute(value, axis, SWAP)


def from_ahead(value, axis, distance):
    return lax.ppermute(value, axis, [(i, (i - distance) % RING) for i in range(RING)])


def to_ahead(value, axis, distance):
    return lax.ppermute(value, axis, [(i, (i + distance) % RING) for i in range(RING)])


def ring_pieces(value, axis):
    return [value] + [from_ahead(value, axis, k) for k in range(1, RING)]


def pair(axis, value, first):
    other = [1, 0, 3, 2] if first else [3, 2, 1, 0]
    return lax.ppermute(value, axis, list(enumerate(other)))


def line_gather(value):
    two = jnp.stack([value, pair(Z, value, True)])
    return jnp.concatenate([two, pair(Z, two, False)])


def line_slot(tile_z, z):
    return jnp.where(
        tile_z == z, 0, jnp.where(tile_z == (z ^ 1), 1, jnp.where(tile_z == 3 - z, 2, 3))
    )


def place(tile, where):
    return tile - tile % RING + line_slot(tile % RING, where[2])


def pick_kernel(where, own_ids, other_ids, gathered, own_ref, other_ref):
    for ids, out in ((other_ids, other_ref), (own_ids, own_ref)):
        for j in range(ids.shape[1]):
            out[j] = gathered[place(ids[0, j], where)]


def scenario_kernel(
    where, own_picked, other_picked, border_own, border_other, inverse_own, inverse_other,
    keep_ref, send_ref, picked, values,
):
    core, side = where[3], where[4]
    half_rows = border_own.shape[0]
    tiles = own_picked.shape[0]
    for j in range(tiles):
        picked[pl.ds(pl.multiple_of(j * TILE + core * HALF, HALF), HALF), :] = own_picked[j]
        picked[pl.ds(pl.multiple_of(j * TILE + (1 - core) * HALF, HALF), HALF), :] = other_picked[j]
    rows = lax.broadcasted_iota(jnp.int32, (half_rows, values.shape[1]), 0)
    own_start = pl.multiple_of(side * half_rows, half_rows)
    other_start = pl.multiple_of((1 - side) * half_rows, half_rows)
    live = where[5]

    def masked(product, start):
        return jnp.where(rows + start < live, product, 0.0).astype(BF16)

    whole = picked[...]
    values[pl.ds(own_start, half_rows), :] = masked(
        jnp.dot(border_own[...], whole, preferred_element_type=F32), own_start
    )
    values[pl.ds(other_start, half_rows), :] = masked(
        jnp.dot(border_other[...], whole, preferred_element_type=F32), other_start
    )
    operand = values[...]
    solved_own = masked(jnp.dot(inverse_own[...], operand, preferred_element_type=F32), own_start)
    solved_other = masked(jnp.dot(inverse_other[...], operand, preferred_element_type=F32), other_start)
    numbers = (((0,), (0,)), ((), ()))
    term = lax.dot_general(border_own[...], solved_own, numbers, preferred_element_type=F32)
    term += lax.dot_general(border_other[...], solved_other, numbers, preferred_element_type=F32)
    term = term.reshape(tiles, 2, HALF, term.shape[1])

    @pl.when(core == 0)
    def _():
        keep_ref[...] = term[:, 0]
        send_ref[...] = term[:, 1]

    @pl.when(core == 1)
    def _():
        keep_ref[...] = term[:, 1]
        send_ref[...] = term[:, 0]


def scatter_kernel(where, own_ids, other_ids, keep, arrived, out, total):
    total[...] = jnp.zeros_like(total)
    for ids, terms in ((own_ids, keep), (other_ids, arrived)):
        for j in range(ids.shape[1]):
            total[place(ids[0, j], where)] += terms[j]
    out[...] = total[...].astype(BF16)


def update_kernel(where, start, precond, b1, b2, b3, *refs):
    pieces, (o0, o1, o2, o3, whole) = refs[:8], refs[8:]
    y, x, z, core = where[0], where[1], where[2], where[3]
    slots = (z, z ^ 1, 3 - z, (3 - z) ^ 1)
    for side in range(2):
        half = core if side == 0 else 1 - core
        for i in range(RING):
            piece = pieces[side * RING + i]
            base = ((x + i) % RING) * 4
            for j in range(RING):
                at = pl.multiple_of((base + slots[j]) * TILE + half * HALF, HALF)
                whole[pl.ds(at, HALF), :] = piece[j]
    operand = whole[...]
    span = operand.shape[0]
    own = precond[:, pl.ds(pl.multiple_of(y * span, span), span)]
    o0[...] = start[...] + jnp.dot(own, operand, preferred_element_type=F32)
    for block, out in ((b1, o1), (b2, o2), (b3, o3)):
        out[...] = jnp.dot(block[...], operand, preferred_element_type=F32)


def call(kernel, specs, outs, scratch=(), flops=0, moved=0):
    return pl.pallas_call(
        kernel,
        out_shape=outs,
        in_specs=specs,
        out_specs=jax.tree.map(lambda _: VMEM, outs),
        scratch_shapes=scratch,
        cost_estimate=pl.CostEstimate(flops=flops, bytes_accessed=moved, transcendentals=0),
        compiler_params=pltpu.CompilerParams(vmem_limit_bytes=32 * 1024 * 1024),
    )


def local(
    start_guess,
    right_side,
    root_diagonal,
    preconditioner,
    border_block,
    coupling_inverse,
    border_count,
    column_tiles,
):
    rows, cols = start_guess.shape
    shape = jax.ShapeDtypeStruct
    where = jnp.stack(
        [*(lax.axis_index(a).astype(jnp.int32) for a in (Y, X, Z, CORE, SIDE)), border_count[0]]
    )
    border, inverse = border_block[0], coupling_inverse[0]
    tiles = column_tiles.shape[1]
    everywhere = RING * RING * RING

    line = line_gather(start_guess.astype(BF16))
    span = preconditioner.shape[1] // RING

    def for_ahead(k):
        first = ((where[0] + k) % RING) * span
        return lax.dynamic_slice_in_dim(preconditioner, first, span, 1)

    block1 = to_ahead(for_ahead(1), Y, 1)
    line, block1, border_late, inverse_late = lax.optimization_barrier((line, block1, border, inverse))
    border_other = swap(border_late, SIDE)
    inverse_other = swap(inverse_late, SIDE)
    other_tiles = swap(column_tiles, CORE)
    copies = jnp.broadcast_to(line, (RING * RING, *line.shape))
    gathered = lax.all_to_all(copies, (Y, X), 0, 0, tiled=True)

    own_half, for_other = call(
        pick_kernel,
        [SMEM] * 3 + [VMEM],
        [shape((tiles, HALF, cols), BF16)] * 2,
    )(where, column_tiles, other_tiles, gathered.reshape(everywhere, HALF, cols))
    other_half = swap(for_other, CORE)
    gate, columns3 = lax.optimization_barrier((own_half, for_ahead(3)))
    block3 = to_ahead(columns3, Y, 3)
    keep, send = call(
        scenario_kernel,
        [SMEM] + [VMEM] * 6,
        [shape((tiles, HALF, cols), F32)] * 2,
        [pltpu.VMEM((tiles * TILE, cols), BF16), pltpu.VMEM((2 * border.shape[0], cols), BF16)],
    )(where, gate, other_half, border, border_other, inverse, inverse_other)
    arrived = swap(send, CORE)
    spread = call(
        scatter_kernel,
        [SMEM] * 3 + [VMEM] * 2,
        shape((everywhere, HALF, cols), BF16),
        [pltpu.VMEM((everywhere, HALF, cols), F32)],
    )(where, column_tiles, other_tiles, keep, arrived)
    spread, block3 = lax.optimization_barrier((spread, block3))
    terms = lax.all_to_all(spread.reshape(RING * RING, RING, HALF, cols), (Y, X), 0, 0, tiled=True)
    line = terms.astype(F32).sum(axis=0)
    columns2, line = lax.optimization_barrier((for_ahead(2), line))
    block2 = to_ahead(columns2, Y, 2)
    own_terms = right_side - root_diagonal[:, None] * start_guess
    line = line + jnp.concatenate([own_terms[None], jnp.zeros_like(line[1:])])
    met = pair(Z, line.astype(BF16), True).astype(F32)
    line = line + jnp.stack([met[1], met[0], met[3], met[2]])
    met = pair(Z, line.astype(BF16), False).astype(F32)
    line = line + jnp.concatenate([met[2:], met[:2]])

    mine = ring_pieces(line.astype(BF16), X)
    partners = [swap(piece, CORE) for piece in mine]
    parts = call(
        update_kernel,
        [SMEM] + [VMEM] * 13,
        [shape((rows, cols), F32)] * RING,
        [pltpu.VMEM((span, cols), BF16)],
    )(where, start_guess, preconditioner, block1, block2, block3, *mine, *partners)
    out = parts[0]
    for k in range(1, RING):
        out = out + from_ahead(parts[k], Y, k)
    return out


def solution(mesh):
    torus = Mesh(
        mesh.devices.reshape(RING, RING, RING, mesh.shape["rootr"], mesh.shape["rootc"]),
        (Y, X, Z, CORE, SIDE),
    )
    in_specs = (
        P(SCEN_ROOTR, SIDE),
        P(SCEN_ROOTR, SIDE),
        P(SCEN_ROOTR),
        P(SCEN_ROOTR, None),
        P(SCEN_ROOTR, SIDE, None),
        P(SCEN_ROOTR, SIDE, None),
        P(SCEN_ROOTR),
        P(SCEN_ROOTR, None),
    )
    return jax.shard_map(
        local, mesh=torus, in_specs=in_specs, out_specs=P(SCEN_ROOTR, SIDE), check_vma=False
    )
```

```python
import functools

import jax
import jax.numpy as jnp
from jax import lax
from jax.experimental import pallas as pl
from jax.experimental.pallas import tpu as pltpu
from jax.sharding import Mesh
from jax.sharding import PartitionSpec as P

TILE = 128
HALF = 64
RING = 4
Y, X, Z, CORE, SIDE = "scen_0", "scen_1", "scen_2", "rootr", "rootc"
SCEN_ROOTR = (Y, X, Z, CORE)
SWAP = [(0, 1), (1, 0)]
F32 = jnp.float32
BF16 = jnp.bfloat16

VMEM = pl.BlockSpec(memory_space=pltpu.VMEM)
SMEM = pl.BlockSpec(memory_space=pltpu.SMEM)


def swap(value, axis):
    return lax.ppermute(value, axis, SWAP)


def from_ahead(value, axis, distance):
    return lax.ppermute(value, axis, [(i, (i - distance) % RING) for i in range(RING)])


def to_ahead(value, axis, distance):
    return lax.ppermute(value, axis, [(i, (i + distance) % RING) for i in range(RING)])


def ring_pieces(value, axis):
    return [value] + [from_ahead(value, axis, k) for k in range(1, RING)]


def pair(axis, value, first):
    other = [1, 0, 3, 2] if first else [3, 2, 1, 0]
    return lax.ppermute(value, axis, list(enumerate(other)))


def line_gather(value):
    two = jnp.stack([value, pair(Z, value, True)])
    return jnp.concatenate([two, pair(Z, two, False)])


def line_slot(tile_z, z):
    return jnp.where(
        tile_z == z, 0, jnp.where(tile_z == (z ^ 1), 1, jnp.where(tile_z == 3 - z, 2, 3))
    )


def place(tile, where):
    return tile - tile % RING + line_slot(tile % RING, where[2])


def pick_kernel(where, own_ids, other_ids, gathered, own_ref, other_ref):
    for ids, out in ((other_ids, other_ref), (own_ids, own_ref)):
        for j in range(ids.shape[1]):
            out[j] = gathered[place(ids[0, j], where)]


def scenario_kernel(
    where, own_picked, other_picked, border_own, border_other, inverse_own, inverse_other,
    keep_ref, send_ref, picked, values,
):
    core, side = where[3], where[4]
    half_rows = border_own.shape[0]
    tiles = own_picked.shape[0]
    for j in range(tiles):
        picked[pl.ds(pl.multiple_of(j * TILE + core * HALF, HALF), HALF), :] = own_picked[j]
        picked[pl.ds(pl.multiple_of(j * TILE + (1 - core) * HALF, HALF), HALF), :] = other_picked[j]
    rows = lax.broadcasted_iota(jnp.int32, (half_rows, values.shape[1]), 0)
    own_start = pl.multiple_of(side * half_rows, half_rows)
    other_start = pl.multiple_of((1 - side) * half_rows, half_rows)
    live = where[5]

    def masked(product, start):
        return jnp.where(rows + start < live, product, 0.0).astype(BF16)

    whole = picked[...]
    values[pl.ds(own_start, half_rows), :] = masked(
        jnp.dot(border_own[...], whole, preferred_element_type=F32), own_start
    )
    values[pl.ds(other_start, half_rows), :] = masked(
        jnp.dot(border_other[...], whole, preferred_element_type=F32), other_start
    )
    operand = values[...]
    solved_own = masked(jnp.dot(inverse_own[...], operand, preferred_element_type=F32), own_start)
    solved_other = masked(jnp.dot(inverse_other[...], operand, preferred_element_type=F32), other_start)
    numbers = (((0,), (0,)), ((), ()))
    term = lax.dot_general(border_own[...], solved_own, numbers, preferred_element_type=F32)
    term += lax.dot_general(border_other[...], solved_other, numbers, preferred_element_type=F32)
    term = term.reshape(tiles, 2, HALF, term.shape[1])

    @pl.when(core == 0)
    def _():
        keep_ref[...] = term[:, 0]
        send_ref[...] = term[:, 1]

    @pl.when(core == 1)
    def _():
        keep_ref[...] = term[:, 1]
        send_ref[...] = term[:, 0]


def scatter_kernel(where, own_ids, other_ids, keep, arrived, out, total):
    total[...] = jnp.zeros_like(total)
    for ids, terms in ((own_ids, keep), (other_ids, arrived)):
        for j in range(ids.shape[1]):
            total[place(ids[0, j], where)] += terms[j]
    out[...] = total[...].astype(BF16)


def update_kernel(where, start, precond, b1, b2, b3, *refs):
    pieces, (o0, o1, o2, o3, whole) = refs[:8], refs[8:]
    y, x, z, core = where[0], where[1], where[2], where[3]
    slots = (z, z ^ 1, 3 - z, (3 - z) ^ 1)
    for side in range(2):
        half = core if side == 0 else 1 - core
        for i in range(RING):
            piece = pieces[side * RING + i]
            base = ((x + i) % RING) * 4
            for j in range(RING):
                at = pl.multiple_of((base + slots[j]) * TILE + half * HALF, HALF)
                whole[pl.ds(at, HALF), :] = piece[j]
    operand = whole[...]
    span = operand.shape[0]
    own = precond[:, pl.ds(pl.multiple_of(y * span, span), span)]
    o0[...] = start[...] + jnp.dot(own, operand, preferred_element_type=F32)
    for block, out in ((b1, o1), (b2, o2), (b3, o3)):
        out[...] = jnp.dot(block[...], operand, preferred_element_type=F32)


def call(kernel, specs, outs, scratch=(), flops=0, moved=0):
    return pl.pallas_call(
        kernel,
        out_shape=outs,
        in_specs=specs,
        out_specs=jax.tree.map(lambda _: VMEM, outs),
        scratch_shapes=scratch,
        cost_estimate=pl.CostEstimate(flops=flops, bytes_accessed=moved, transcendentals=0),
        compiler_params=pltpu.CompilerParams(vmem_limit_bytes=32 * 1024 * 1024),
    )


def local(
    start_guess,
    right_side,
    root_diagonal,
    preconditioner,
    border_block,
    coupling_inverse,
    border_count,
    column_tiles,
):
    rows, cols = start_guess.shape
    shape = jax.ShapeDtypeStruct
    where = jnp.stack(
        [*(lax.axis_index(a).astype(jnp.int32) for a in (Y, X, Z, CORE, SIDE)), border_count[0]]
    )
    border, inverse = border_block[0], coupling_inverse[0]
    tiles = column_tiles.shape[1]
    everywhere = RING * RING * RING

    line = line_gather(start_guess.astype(BF16))
    span = preconditioner.shape[1] // RING

    line, late, border_late, inverse_late = lax.optimization_barrier(
        (line, preconditioner, border, inverse)
    )
    columns = [
        lax.dynamic_slice_in_dim(late, ((where[0] + k) % RING) * span, span, 1)
        for k in range(1, RING)
    ]
    block1, block3 = to_ahead(columns[0], Y, 1), to_ahead(columns[2], Y, 3)
    border_other = swap(border_late, SIDE)
    inverse_other = swap(inverse_late, SIDE)
    other_tiles = swap(column_tiles, CORE)
    copies = jnp.broadcast_to(line, (RING * RING, *line.shape))
    gathered = lax.all_to_all(copies, (Y, X), 0, 0, tiled=True)
    gathered, block1, block3 = lax.optimization_barrier((gathered, block1, block3))

    own_half, for_other = call(
        pick_kernel,
        [SMEM] * 3 + [VMEM],
        [shape((tiles, HALF, cols), BF16)] * 2,
    )(where, column_tiles, other_tiles, gathered.reshape(everywhere, HALF, cols))
    other_half = swap(for_other, CORE)
    own_half, columns2 = lax.optimization_barrier((own_half, columns[1]))
    block2 = to_ahead(columns2, Y, 2)
    keep, send = call(
        scenario_kernel,
        [SMEM] + [VMEM] * 6,
        [shape((tiles, HALF, cols), F32)] * 2,
        [pltpu.VMEM((tiles * TILE, cols), BF16), pltpu.VMEM((2 * border.shape[0], cols), BF16)],
    )(where, own_half, other_half, border, border_other, inverse, inverse_other)
    arrived = swap(send, CORE)
    spread = call(
        scatter_kernel,
        [SMEM] * 3 + [VMEM] * 2,
        shape((everywhere, HALF, cols), BF16),
        [pltpu.VMEM((everywhere, HALF, cols), F32)],
    )(where, column_tiles, other_tiles, keep, arrived)
    terms = lax.all_to_all(spread.reshape(RING * RING, RING, HALF, cols), (Y, X), 0, 0, tiled=True)
    terms, block2 = lax.optimization_barrier((terms, block2))
    line = terms.astype(F32).sum(axis=0)
    own_terms = right_side - root_diagonal[:, None] * start_guess
    line = line + jnp.concatenate([own_terms[None], jnp.zeros_like(line[1:])])
    met = pair(Z, line.astype(BF16), True).astype(F32)
    line = line + jnp.stack([met[1], met[0], met[3], met[2]])
    met = pair(Z, line.astype(BF16), False).astype(F32)
    line = line + jnp.concatenate([met[2:], met[:2]])

    mine = ring_pieces(line.astype(BF16), X)
    partners = [swap(piece, CORE) for piece in mine]
    parts = call(
        update_kernel,
        [SMEM] + [VMEM] * 13,
        [shape((rows, cols), F32)] * RING,
        [pltpu.VMEM((span, cols), BF16)],
    )(where, start_guess, preconditioner, block1, block2, block3, *mine, *partners)
    out = parts[0]
    for k in range(1, RING):
        out = out + from_ahead(parts[k], Y, k)
    return out


def solution(mesh):
    torus = Mesh(
        mesh.devices.reshape(RING, RING, RING, mesh.shape["rootr"], mesh.shape["rootc"]),
        (Y, X, Z, CORE, SIDE),
    )
    in_specs = (
        P(SCEN_ROOTR, SIDE),
        P(SCEN_ROOTR, SIDE),
        P(SCEN_ROOTR),
        P(SCEN_ROOTR, None),
        P(SCEN_ROOTR, SIDE, None),
        P(SCEN_ROOTR, SIDE, None),
        P(SCEN_ROOTR),
        P(SCEN_ROOTR, None),
    )
    return jax.shard_map(
        local, mesh=torus, in_specs=in_specs, out_specs=P(SCEN_ROOTR, SIDE), check_vma=False
    )
```

```python
import functools

import jax
import jax.numpy as jnp
from jax import lax
from jax.experimental import pallas as pl
from jax.experimental.pallas import tpu as pltpu
from jax.sharding import Mesh
from jax.sharding import PartitionSpec as P

TILE = 128
HALF = 64
RING = 4
Y, X, Z, CORE, SIDE = "scen_0", "scen_1", "scen_2", "rootr", "rootc"
SCEN_ROOTR = (Y, X, Z, CORE)
SWAP = [(0, 1), (1, 0)]
F32 = jnp.float32
BF16 = jnp.bfloat16

VMEM = pl.BlockSpec(memory_space=pltpu.VMEM)
SMEM = pl.BlockSpec(memory_space=pltpu.SMEM)


def swap(value, axis):
    return lax.ppermute(value, axis, SWAP)


def to_ahead(value, axis, distance):
    return lax.ppermute(value, axis, [(i, (i + distance) % RING) for i in range(RING)])


def exchange(pieces, axes):
    return lax.all_to_all(pieces, axes, 0, 0, tiled=True)


def everyones(value, axes, count):
    return exchange(jnp.broadcast_to(value, (count, *value.shape)), axes)


def pick_kernel(own_ids, other_ids, gathered, own_ref, other_ref):
    for ids, out in ((other_ids, other_ref), (own_ids, own_ref)):
        for j in range(ids.shape[1]):
            out[j] = gathered[ids[0, j]]


def scenario_kernel(
    where, own_picked, other_picked, border_own, border_other, inverse_own, inverse_other,
    keep_ref, send_ref, picked, values,
):
    core, side = where[3], where[4]
    half_rows = border_own.shape[0]
    tiles = own_picked.shape[0]
    for j in range(tiles):
        picked[pl.ds(pl.multiple_of(j * TILE + core * HALF, HALF), HALF), :] = own_picked[j]
        picked[pl.ds(pl.multiple_of(j * TILE + (1 - core) * HALF, HALF), HALF), :] = other_picked[j]
    rows = lax.broadcasted_iota(jnp.int32, (half_rows, values.shape[1]), 0)
    own_start = pl.multiple_of(side * half_rows, half_rows)
    other_start = pl.multiple_of((1 - side) * half_rows, half_rows)
    live = where[5]

    def masked(product, start):
        return jnp.where(rows + start < live, product, 0.0).astype(BF16)

    whole = picked[...]
    values[pl.ds(own_start, half_rows), :] = masked(
        jnp.dot(border_own[...], whole, preferred_element_type=F32), own_start
    )
    values[pl.ds(other_start, half_rows), :] = masked(
        jnp.dot(border_other[...], whole, preferred_element_type=F32), other_start
    )
    operand = values[...]
    solved_own = masked(jnp.dot(inverse_own[...], operand, preferred_element_type=F32), own_start)
    solved_other = masked(jnp.dot(inverse_other[...], operand, preferred_element_type=F32), other_start)
    numbers = (((0,), (0,)), ((), ()))
    term = lax.dot_general(border_own[...], solved_own, numbers, preferred_element_type=F32)
    term += lax.dot_general(border_other[...], solved_other, numbers, preferred_element_type=F32)
    term = term.reshape(tiles, 2, HALF, term.shape[1])

    @pl.when(core == 0)
    def _():
        keep_ref[...] = term[:, 0]
        send_ref[...] = term[:, 1]

    @pl.when(core == 1)
    def _():
        keep_ref[...] = term[:, 1]
        send_ref[...] = term[:, 0]


def scatter_kernel(own_ids, other_ids, keep, arrived, out, total):
    total[...] = jnp.zeros_like(total)
    for ids, terms in ((own_ids, keep), (other_ids, arrived)):
        for j in range(ids.shape[1]):
            total[ids[0, j]] += terms[j]
    out[...] = total[...].astype(BF16)


def update_kernel(where, start, precond, b1, b2, b3, mine, partners, out, whole):
    y, core = where[0], where[3]
    for side, piece in enumerate((mine, partners)):
        half = core if side == 0 else 1 - core
        for tile in range(piece.shape[0]):
            at = pl.multiple_of(tile * TILE + half * HALF, HALF)
            whole[pl.ds(at, HALF), :] = piece[tile]
    operand = whole[...]
    span = operand.shape[0]
    own = precond[:, pl.ds(pl.multiple_of(y * span, span), span)]
    out[y] = start[...] + jnp.dot(own, operand, preferred_element_type=F32)
    for k, block in enumerate((b1, b2, b3)):
        out[(y + RING - 1 - k) % RING] = jnp.dot(block[...], operand, preferred_element_type=F32)


def call(kernel, specs, outs, scratch=(), flops=0, moved=0):
    return pl.pallas_call(
        kernel,
        out_shape=outs,
        in_specs=specs,
        out_specs=jax.tree.map(lambda _: VMEM, outs),
        scratch_shapes=scratch,
        cost_estimate=pl.CostEstimate(flops=flops, bytes_accessed=moved, transcendentals=0),
        compiler_params=pltpu.CompilerParams(vmem_limit_bytes=32 * 1024 * 1024),
    )


def local(
    start_guess,
    right_side,
    root_diagonal,
    preconditioner,
    border_block,
    coupling_inverse,
    border_count,
    column_tiles,
):
    rows, cols = start_guess.shape
    shape = jax.ShapeDtypeStruct
    where = jnp.stack(
        [*(lax.axis_index(a).astype(jnp.int32) for a in (Y, X, Z, CORE, SIDE)), border_count[0]]
    )
    border, inverse = border_block[0], coupling_inverse[0]
    tiles = column_tiles.shape[1]
    everywhere = RING * RING * RING

    line = everyones(start_guess.astype(BF16), Z, RING)
    span = preconditioner.shape[1] // RING

    def for_ahead(k):
        first = ((where[0] + k) % RING) * span
        return lax.dynamic_slice_in_dim(preconditioner, first, span, 1)

    block1, block3 = to_ahead(for_ahead(1), Y, 1), to_ahead(for_ahead(3), Y, 3)
    line, block1, block3, border_late, inverse_late = lax.optimization_barrier(
        (line, block1, block3, border, inverse)
    )
    border_other = swap(border_late, SIDE)
    inverse_other = swap(inverse_late, SIDE)
    other_tiles = swap(column_tiles, CORE)
    gathered = everyones(line, (Y, X), RING * RING)

    own_half, for_other = call(
        pick_kernel,
        [SMEM] * 2 + [VMEM],
        [shape((tiles, HALF, cols), BF16)] * 2,
    )(column_tiles, other_tiles, gathered.reshape(everywhere, HALF, cols))
    other_half = swap(for_other, CORE)
    keep, send = call(
        scenario_kernel,
        [SMEM] + [VMEM] * 6,
        [shape((tiles, HALF, cols), F32)] * 2,
        [pltpu.VMEM((tiles * TILE, cols), BF16), pltpu.VMEM((2 * border.shape[0], cols), BF16)],
    )(where, own_half, other_half, border, border_other, inverse, inverse_other)
    arrived = swap(send, CORE)
    spread = call(
        scatter_kernel,
        [SMEM] * 2 + [VMEM] * 2,
        shape((everywhere, HALF, cols), BF16),
        [pltpu.VMEM((everywhere, HALF, cols), F32)],
    )(column_tiles, other_tiles, keep, arrived)
    terms = exchange(spread.reshape(RING * RING, RING, HALF, cols), (Y, X))
    line = terms.astype(F32).sum(axis=0)
    columns2, line = lax.optimization_barrier((for_ahead(2), line))
    block2 = to_ahead(columns2, Y, 2)
    own_terms = right_side - root_diagonal[:, None] * start_guess
    mine_here = (jnp.arange(RING) == where[2])[:, None, None]
    line = line + jnp.where(mine_here, own_terms, 0.0)
    line = everyones(line.astype(BF16), Z, RING).astype(F32).sum(axis=0)

    mine = everyones(line.astype(BF16), X, RING).reshape(RING * RING, HALF, cols)
    partners = swap(mine, CORE)
    parts = call(
        update_kernel,
        [SMEM] + [VMEM] * 7,
        shape((RING, rows, cols), F32),
        [pltpu.VMEM((span, cols), BF16)],
    )(where, start_guess, preconditioner, block1, block2, block3, mine, partners)
    return exchange(parts, Y).sum(axis=0)


def solution(mesh):
    torus = Mesh(
        mesh.devices.reshape(RING, RING, RING, mesh.shape["rootr"], mesh.shape["rootc"]),
        (Y, X, Z, CORE, SIDE),
    )
    in_specs = (
        P(SCEN_ROOTR, SIDE),
        P(SCEN_ROOTR, SIDE),
        P(SCEN_ROOTR),
        P(SCEN_ROOTR, None),
        P(SCEN_ROOTR, SIDE, None),
        P(SCEN_ROOTR, SIDE, None),
        P(SCEN_ROOTR),
        P(SCEN_ROOTR, None),
    )
    return jax.shard_map(
        local, mesh=torus, in_specs=in_specs, out_specs=P(SCEN_ROOTR, SIDE), check_vma=False
    )
```

```python
import functools

import jax
import jax.numpy as jnp
from jax import lax
from jax.experimental import pallas as pl
from jax.experimental.pallas import tpu as pltpu
from jax.sharding import Mesh
from jax.sharding import PartitionSpec as P

TILE = 128
HALF = 64
RING = 4
Y, X, Z, CORE, SIDE = "scen_0", "scen_1", "scen_2", "rootr", "rootc"
SCEN_ROOTR = (Y, X, Z, CORE)
SWAP = [(0, 1), (1, 0)]
F32 = jnp.float32
BF16 = jnp.bfloat16

VMEM = pl.BlockSpec(memory_space=pltpu.VMEM)
SMEM = pl.BlockSpec(memory_space=pltpu.SMEM)


def swap(value, axis):
    return lax.ppermute(value, axis, SWAP)


def from_ahead(value, axis, distance):
    return lax.ppermute(value, axis, [(i, (i - distance) % RING) for i in range(RING)])


def to_ahead(value, axis, distance):
    return lax.ppermute(value, axis, [(i, (i + distance) % RING) for i in range(RING)])


def ring_pieces(value, axis):
    return [value] + [from_ahead(value, axis, k) for k in range(1, RING)]


def pair(axis, value, first):
    other = [1, 0, 3, 2] if first else [3, 2, 1, 0]
    return lax.ppermute(value, axis, list(enumerate(other)))


def line_gather(value):
    two = jnp.stack([value, pair(Z, value, True)])
    return jnp.concatenate([two, pair(Z, two, False)])


def line_slot(tile_z, z):
    return jnp.where(
        tile_z == z, 0, jnp.where(tile_z == (z ^ 1), 1, jnp.where(tile_z == 3 - z, 2, 3))
    )


def place(tile, where):
    return tile - tile % RING + line_slot(tile % RING, where[2])


def pick_kernel(where, own_ids, other_ids, gathered, own_ref, other_ref):
    for ids, out in ((other_ids, other_ref), (own_ids, own_ref)):
        for j in range(ids.shape[1]):
            out[j] = gathered[place(ids[0, j], where)]


def scenario_kernel(
    where, own_picked, other_picked, border_own, border_other, inverse_own, inverse_other,
    keep_ref, send_ref, picked, values,
):
    core, side = where[3], where[4]
    half_rows = border_own.shape[0]
    tiles = own_picked.shape[0]
    for j in range(tiles):
        picked[pl.ds(pl.multiple_of(j * TILE + core * HALF, HALF), HALF), :] = own_picked[j]
        picked[pl.ds(pl.multiple_of(j * TILE + (1 - core) * HALF, HALF), HALF), :] = other_picked[j]
    rows = lax.broadcasted_iota(jnp.int32, (half_rows, values.shape[1]), 0)
    own_start = pl.multiple_of(side * half_rows, half_rows)
    other_start = pl.multiple_of((1 - side) * half_rows, half_rows)
    live = where[5]

    def masked(product, start):
        return jnp.where(rows + start < live, product, 0.0).astype(BF16)

    whole = picked[...]
    values[pl.ds(own_start, half_rows), :] = masked(
        jnp.dot(border_own[...], whole, preferred_element_type=F32), own_start
    )
    values[pl.ds(other_start, half_rows), :] = masked(
        jnp.dot(border_other[...], whole, preferred_element_type=F32), other_start
    )
    operand = values[...]
    solved_own = masked(jnp.dot(inverse_own[...], operand, preferred_element_type=F32), own_start)
    solved_other = masked(jnp.dot(inverse_other[...], operand, preferred_element_type=F32), other_start)
    numbers = (((0,), (0,)), ((), ()))
    term = lax.dot_general(border_own[...], solved_own, numbers, preferred_element_type=F32)
    term += lax.dot_general(border_other[...], solved_other, numbers, preferred_element_type=F32)
    term = term.reshape(tiles, 2, HALF, term.shape[1])

    @pl.when(core == 0)
    def _():
        keep_ref[...] = term[:, 0]
        send_ref[...] = term[:, 1]

    @pl.when(core == 1)
    def _():
        keep_ref[...] = term[:, 1]
        send_ref[...] = term[:, 0]


def scatter_kernel(where, own_ids, other_ids, keep, arrived, out, total):
    total[...] = jnp.zeros_like(total)
    for ids, terms in ((own_ids, keep), (other_ids, arrived)):
        for j in range(ids.shape[1]):
            total[place(ids[0, j], where)] += terms[j]
    out[...] = total[...].astype(BF16)


def update_kernel(where, start, precond, here, there, mine, partners, o0, o1, o2, o3, whole):
    y, x, z, core, side = where[0], where[1], where[2], where[3], where[4]
    slots = (z, z ^ 1, 3 - z, (3 - z) ^ 1)
    for which, plane in enumerate((mine, partners)):
        half = core if which == 0 else 1 - core
        for i in range(RING):
            base = ((x + i) % RING) * 4
            for j in range(RING):
                at = pl.multiple_of((base + slots[j]) * TILE + half * HALF, HALF)
                whole[pl.ds(at, HALF), :] = plane[i * RING + j]
    span = whole.shape[0]
    own = precond[:, pl.ds(pl.multiple_of(y * span, span), span)]
    o0[...] = start[...] + jnp.dot(own, whole[...], preferred_element_type=F32)
    part = span // 2
    ours = whole[pl.ds(pl.multiple_of(side * part, part), part), :]
    theirs = whole[pl.ds(pl.multiple_of((1 - side) * part, part), part), :]
    for k, out in enumerate((o1, o2, o3)):
        out[...] = jnp.dot(here[k], ours, preferred_element_type=F32) + jnp.dot(
            there[k], theirs, preferred_element_type=F32
        )


def call(kernel, specs, outs, scratch=(), flops=0, moved=0):
    return pl.pallas_call(
        kernel,
        out_shape=outs,
        in_specs=specs,
        out_specs=jax.tree.map(lambda _: VMEM, outs),
        scratch_shapes=scratch,
        cost_estimate=pl.CostEstimate(flops=flops, bytes_accessed=moved, transcendentals=0),
        compiler_params=pltpu.CompilerParams(vmem_limit_bytes=32 * 1024 * 1024),
    )


def local(
    start_guess,
    right_side,
    root_diagonal,
    preconditioner,
    border_block,
    coupling_inverse,
    border_count,
    column_tiles,
):
    rows, cols = start_guess.shape
    shape = jax.ShapeDtypeStruct
    where = jnp.stack(
        [*(lax.axis_index(a).astype(jnp.int32) for a in (Y, X, Z, CORE, SIDE)), border_count[0]]
    )
    border, inverse = border_block[0], coupling_inverse[0]
    tiles = column_tiles.shape[1]
    everywhere = RING * RING * RING

    span = preconditioner.shape[1] // RING
    part = span // 2

    def for_ahead(source, k):
        first = ((where[0] + k) % RING) * span + where[4] * part
        return lax.dynamic_slice_in_dim(source, first, part, 1)

    low = start_guess.astype(BF16)
    two = jnp.stack([low, pair(Z, low, True)])
    block1, block3 = to_ahead(for_ahead(preconditioner, 1), Y, 1), to_ahead(for_ahead(preconditioner, 3), Y, 3)
    two, late = lax.optimization_barrier((two, for_ahead(preconditioner, 2)))
    line = jnp.concatenate([two, pair(Z, two, False)])
    block2 = to_ahead(late, Y, 2)
    line, block1, block2, block3, border_late, inverse_late = lax.optimization_barrier(
        (line, block1, block2, block3, border, inverse)
    )
    here = jnp.stack([block1, block2, block3])
    border_other = swap(border_late, SIDE)
    inverse_other = swap(inverse_late, SIDE)
    there = swap(here, SIDE)
    other_tiles = swap(column_tiles, CORE)
    copies = jnp.broadcast_to(line, (RING * RING, *line.shape))
    gathered = lax.all_to_all(copies, (Y, X), 0, 0, tiled=True)

    own_half, for_other = call(
        pick_kernel,
        [SMEM] * 3 + [VMEM],
        [shape((tiles, HALF, cols), BF16)] * 2,
    )(where, column_tiles, other_tiles, gathered.reshape(everywhere, HALF, cols))
    other_half = swap(for_other, CORE)
    keep, send = call(
        scenario_kernel,
        [SMEM] + [VMEM] * 6,
        [shape((tiles, HALF, cols), F32)] * 2,
        [pltpu.VMEM((tiles * TILE, cols), BF16), pltpu.VMEM((2 * border.shape[0], cols), BF16)],
    )(where, own_half, other_half, border, border_other, inverse, inverse_other)
    arrived = swap(send, CORE)
    spread = call(
        scatter_kernel,
        [SMEM] * 3 + [VMEM] * 2,
        shape((everywhere, HALF, cols), BF16),
        [pltpu.VMEM((everywhere, HALF, cols), F32)],
    )(where, column_tiles, other_tiles, keep, arrived)
    terms = lax.all_to_all(spread.reshape(RING * RING, RING, HALF, cols), (Y, X), 0, 0, tiled=True)
    terms, there = lax.optimization_barrier((terms, there))
    line = terms.astype(F32).sum(axis=0)
    own_terms = right_side - root_diagonal[:, None] * start_guess
    line = line + jnp.concatenate([own_terms[None], jnp.zeros_like(line[1:])])
    met = pair(Z, line.astype(BF16), True).astype(F32)
    line = line + jnp.stack([met[1], met[0], met[3], met[2]])
    met = pair(Z, line.astype(BF16), False).astype(F32)
    line = line + jnp.concatenate([met[2:], met[:2]])

    mine = jnp.concatenate(ring_pieces(line.astype(BF16), X))
    partners = swap(mine, CORE)
    parts = call(
        update_kernel,
        [SMEM] + [VMEM] * 6,
        [shape((rows, cols), F32)] * RING,
        [pltpu.VMEM((span, cols), BF16)],
    )(where, start_guess, preconditioner, here, there, mine, partners)
    out = parts[0]
    for k in range(1, RING):
        out = out + from_ahead(parts[k], Y, k)
    return out


def solution(mesh):
    torus = Mesh(
        mesh.devices.reshape(RING, RING, RING, mesh.shape["rootr"], mesh.shape["rootc"]),
        (Y, X, Z, CORE, SIDE),
    )
    in_specs = (
        P(SCEN_ROOTR, SIDE),
        P(SCEN_ROOTR, SIDE),
        P(SCEN_ROOTR),
        P(SCEN_ROOTR, None),
        P(SCEN_ROOTR, SIDE, None),
        P(SCEN_ROOTR, SIDE, None),
        P(SCEN_ROOTR),
        P(SCEN_ROOTR, None),
    )
    return jax.shard_map(
        local, mesh=torus, in_specs=in_specs, out_specs=P(SCEN_ROOTR, SIDE), check_vma=False
    )
```

```python
import functools

import jax
import jax.numpy as jnp
from jax import lax
from jax.experimental import pallas as pl
from jax.experimental.pallas import tpu as pltpu
from jax.sharding import Mesh
from jax.sharding import PartitionSpec as P

TILE = 128
HALF = 64
RING = 4
Y, X, Z, CORE, SIDE = "scen_0", "scen_1", "scen_2", "rootr", "rootc"
SCEN_ROOTR = (Y, X, Z, CORE)
SWAP = [(0, 1), (1, 0)]
F32 = jnp.float32
BF16 = jnp.bfloat16

VMEM = pl.BlockSpec(memory_space=pltpu.VMEM)
SMEM = pl.BlockSpec(memory_space=pltpu.SMEM)


def swap(value, axis):
    return lax.ppermute(value, axis, SWAP)


def from_ahead(value, axis, distance):
    return lax.ppermute(value, axis, [(i, (i - distance) % RING) for i in range(RING)])


def to_ahead(value, axis, distance):
    return lax.ppermute(value, axis, [(i, (i + distance) % RING) for i in range(RING)])


def ring_pieces(value, axis):
    return [value] + [from_ahead(value, axis, k) for k in range(1, RING)]


def pair(axis, value, first):
    other = [1, 0, 3, 2] if first else [3, 2, 1, 0]
    return lax.ppermute(value, axis, list(enumerate(other)))


def line_gather(value):
    two = jnp.stack([value, pair(Z, value, True)])
    return jnp.concatenate([two, pair(Z, two, False)])


def line_slot(tile_z, z):
    return jnp.where(
        tile_z == z, 0, jnp.where(tile_z == (z ^ 1), 1, jnp.where(tile_z == 3 - z, 2, 3))
    )


def place(tile, where):
    return tile - tile % RING + line_slot(tile % RING, where[2])


def copies_kernel(line, out, done):
    copies = [pltpu.make_async_copy(line, out.at[k], done.at[k]) for k in range(out.shape[0])]
    for copy in copies:
        copy.start()
    for copy in copies:
        copy.wait()


def pick_kernel(where, own_ids, other_ids, gathered, own_ref, other_ref):
    for ids, out in ((other_ids, other_ref), (own_ids, own_ref)):
        for j in range(ids.shape[1]):
            out[j] = gathered[place(ids[0, j], where)]


def scenario_kernel(
    where, own_picked, other_picked, border_own, border_other, inverse_own, inverse_other,
    keep_ref, send_ref, picked, values,
):
    core, side = where[3], where[4]
    half_rows = border_own.shape[0]
    tiles = own_picked.shape[0]
    for j in range(tiles):
        picked[pl.ds(pl.multiple_of(j * TILE + core * HALF, HALF), HALF), :] = own_picked[j]
        picked[pl.ds(pl.multiple_of(j * TILE + (1 - core) * HALF, HALF), HALF), :] = other_picked[j]
    rows = lax.broadcasted_iota(jnp.int32, (half_rows, values.shape[1]), 0)
    own_start = pl.multiple_of(side * half_rows, half_rows)
    other_start = pl.multiple_of((1 - side) * half_rows, half_rows)
    live = where[5]

    def masked(product, start):
        return jnp.where(rows + start < live, product, 0.0).astype(BF16)

    whole = picked[...]
    values[pl.ds(own_start, half_rows), :] = masked(
        jnp.dot(border_own[...], whole, preferred_element_type=F32), own_start
    )
    values[pl.ds(other_start, half_rows), :] = masked(
        jnp.dot(border_other[...], whole, preferred_element_type=F32), other_start
    )
    operand = values[...]
    solved_own = masked(jnp.dot(inverse_own[...], operand, preferred_element_type=F32), own_start)
    solved_other = masked(jnp.dot(inverse_other[...], operand, preferred_element_type=F32), other_start)
    numbers = (((0,), (0,)), ((), ()))
    term = lax.dot_general(border_own[...], solved_own, numbers, preferred_element_type=F32)
    term += lax.dot_general(border_other[...], solved_other, numbers, preferred_element_type=F32)
    term = term.reshape(tiles, 2, HALF, term.shape[1])

    @pl.when(core == 0)
    def _():
        keep_ref[...] = term[:, 0]
        send_ref[...] = term[:, 1]

    @pl.when(core == 1)
    def _():
        keep_ref[...] = term[:, 1]
        send_ref[...] = term[:, 0]


def scatter_kernel(where, own_ids, other_ids, keep, arrived, out, total):
    both = ((own_ids, keep), (other_ids, arrived))
    spots = [[place(ids[0, j], where) for j in range(ids.shape[1])] for ids, _ in both]
    out[...] = jnp.zeros_like(out)
    for spot in spots[1]:
        total[spot] = jnp.zeros_like(total[spot])
    for j, spot in enumerate(spots[0]):
        total[spot] = keep[j]
    for j, spot in enumerate(spots[1]):
        total[spot] += arrived[j]
    for spot in spots[0] + spots[1]:
        out[spot] = total[spot].astype(BF16)


def update_kernel(where, start, precond, b1, b2, b3, *refs):
    pieces, (o0, o1, o2, o3, whole) = refs[:8], refs[8:]
    y, x, z, core = where[0], where[1], where[2], where[3]
    slots = (z, z ^ 1, 3 - z, (3 - z) ^ 1)
    for side in range(2):
        half = core if side == 0 else 1 - core
        for i in range(RING):
            piece = pieces[side * RING + i]
            base = ((x + i) % RING) * 4
            for j in range(RING):
                at = pl.multiple_of((base + slots[j]) * TILE + half * HALF, HALF)
                whole[pl.ds(at, HALF), :] = piece[j]
    operand = whole[...]
    span = operand.shape[0]
    own = precond[:, pl.ds(pl.multiple_of(y * span, span), span)]
    o0[...] = start[...] + jnp.dot(own, operand, preferred_element_type=F32)
    for block, out in ((b1, o1), (b2, o2), (b3, o3)):
        out[...] = jnp.dot(block[...], operand, preferred_element_type=F32)


def call(kernel, specs, outs, scratch=(), flops=0, moved=0):
    return pl.pallas_call(
        kernel,
        out_shape=outs,
        in_specs=specs,
        out_specs=jax.tree.map(lambda _: VMEM, outs),
        scratch_shapes=scratch,
        cost_estimate=pl.CostEstimate(flops=flops, bytes_accessed=moved, transcendentals=0),
        compiler_params=pltpu.CompilerParams(vmem_limit_bytes=32 * 1024 * 1024),
    )


def local(
    start_guess,
    right_side,
    root_diagonal,
    preconditioner,
    border_block,
    coupling_inverse,
    border_count,
    column_tiles,
):
    rows, cols = start_guess.shape
    shape = jax.ShapeDtypeStruct
    where = jnp.stack(
        [*(lax.axis_index(a).astype(jnp.int32) for a in (Y, X, Z, CORE, SIDE)), border_count[0]]
    )
    border, inverse = border_block[0], coupling_inverse[0]
    tiles = column_tiles.shape[1]
    everywhere = RING * RING * RING

    line = line_gather(start_guess.astype(BF16))
    span = preconditioner.shape[1] // RING

    def for_ahead(k):
        first = ((where[0] + k) % RING) * span
        return lax.dynamic_slice_in_dim(preconditioner, first, span, 1)

    block1 = to_ahead(for_ahead(1), Y, 1)
    line, block1, border_late, inverse_late = lax.optimization_barrier((line, block1, border, inverse))
    border_other = swap(border_late, SIDE)
    inverse_other = swap(inverse_late, SIDE)
    other_tiles = swap(column_tiles, CORE)
    copies = pl.pallas_call(
        copies_kernel,
        out_shape=shape((RING * RING, *line.shape), BF16),
        in_specs=[VMEM],
        out_specs=pl.BlockSpec(memory_space=pl.ANY),
        scratch_shapes=[pltpu.SemaphoreType.DMA((RING * RING,))],
        cost_estimate=pl.CostEstimate(flops=0, bytes_accessed=2**20, transcendentals=0),
    )(line)
    gathered = lax.all_to_all(copies, (Y, X), 0, 0, tiled=True)

    own_half, for_other = call(
        pick_kernel,
        [SMEM] * 3 + [VMEM],
        [shape((tiles, HALF, cols), BF16)] * 2,
    )(where, column_tiles, other_tiles, gathered.reshape(everywhere, HALF, cols))
    other_half = swap(for_other, CORE)
    keep, send = call(
        scenario_kernel,
        [SMEM] + [VMEM] * 6,
        [shape((tiles, HALF, cols), F32)] * 2,
        [pltpu.VMEM((tiles * TILE, cols), BF16), pltpu.VMEM((2 * border.shape[0], cols), BF16)],
    )(where, own_half, other_half, border, border_other, inverse, inverse_other)
    arrived = swap(send, CORE)
    spread = call(
        scatter_kernel,
        [SMEM] * 3 + [VMEM] * 2,
        shape((everywhere, HALF, cols), BF16),
        [pltpu.VMEM((everywhere, HALF, cols), F32)],
    )(where, column_tiles, other_tiles, keep, arrived)
    terms = lax.all_to_all(spread.reshape(RING * RING, RING, HALF, cols), (Y, X), 0, 0, tiled=True)
    line = terms.astype(F32).sum(axis=0)
    columns2, columns3, line = lax.optimization_barrier((for_ahead(2), for_ahead(3), line))
    block2, block3 = to_ahead(columns2, Y, 2), to_ahead(columns3, Y, 3)
    own_terms = right_side - root_diagonal[:, None] * start_guess
    line = line + jnp.concatenate([own_terms[None], jnp.zeros_like(line[1:])])
    met = pair(Z, line.astype(BF16), True).astype(F32)
    line = line + jnp.stack([met[1], met[0], met[3], met[2]])
    met = pair(Z, line.astype(BF16), False).astype(F32)
    line = line + jnp.concatenate([met[2:], met[:2]])

    mine = ring_pieces(line.astype(BF16), X)
    partners = [swap(piece, CORE) for piece in mine]
    parts = call(
        update_kernel,
        [SMEM] + [VMEM] * 13,
        [shape((rows, cols), F32)] * RING,
        [pltpu.VMEM((span, cols), BF16)],
    )(where, start_guess, preconditioner, block1, block2, block3, *mine, *partners)
    out = parts[0]
    for k in range(1, RING):
        out = out + from_ahead(parts[k], Y, k)
    return out


def solution(mesh):
    torus = Mesh(
        mesh.devices.reshape(RING, RING, RING, mesh.shape["rootr"], mesh.shape["rootc"]),
        (Y, X, Z, CORE, SIDE),
    )
    in_specs = (
        P(SCEN_ROOTR, SIDE),
        P(SCEN_ROOTR, SIDE),
        P(SCEN_ROOTR),
        P(SCEN_ROOTR, None),
        P(SCEN_ROOTR, SIDE, None),
        P(SCEN_ROOTR, SIDE, None),
        P(SCEN_ROOTR),
        P(SCEN_ROOTR, None),
    )
    return jax.shard_map(
        local, mesh=torus, in_specs=in_specs, out_specs=P(SCEN_ROOTR, SIDE), check_vma=False
    )
```

```python
import functools

import jax
import jax.numpy as jnp
from jax import lax
from jax.experimental import pallas as pl
from jax.experimental.pallas import tpu as pltpu
from jax.sharding import Mesh
from jax.sharding import PartitionSpec as P

TILE = 128
HALF = 64
RING = 4
Y, X, Z, CORE, SIDE = "scen_0", "scen_1", "scen_2", "rootr", "rootc"
SCEN_ROOTR = (Y, X, Z, CORE)
SWAP = [(0, 1), (1, 0)]
F32 = jnp.float32
BF16 = jnp.bfloat16

VMEM = pl.BlockSpec(memory_space=pltpu.VMEM)
SMEM = pl.BlockSpec(memory_space=pltpu.SMEM)


def swap(value, axis):
    return lax.ppermute(value, axis, SWAP)


def from_ahead(value, axis, distance):
    return lax.ppermute(value, axis, [(i, (i - distance) % RING) for i in range(RING)])


def to_ahead(value, axis, distance):
    return lax.ppermute(value, axis, [(i, (i + distance) % RING) for i in range(RING)])


def ring_pieces(value, axis):
    return [value] + [from_ahead(value, axis, k) for k in range(1, RING)]


def pair(axis, value, first):
    other = [1, 0, 3, 2] if first else [3, 2, 1, 0]
    return lax.ppermute(value, axis, list(enumerate(other)))


def line_gather(value):
    two = jnp.stack([value, pair(Z, value, True)])
    return jnp.concatenate([two, pair(Z, two, False)])


def line_slot(tile_z, z):
    return jnp.where(
        tile_z == z, 0, jnp.where(tile_z == (z ^ 1), 1, jnp.where(tile_z == 3 - z, 2, 3))
    )


def place(tile, where):
    return tile - tile % RING + line_slot(tile % RING, where[2])


def pick_kernel(where, own_ids, other_ids, gathered, own_ref, other_ref):
    for ids, out in ((other_ids, other_ref), (own_ids, own_ref)):
        for j in range(ids.shape[1]):
            out[j] = gathered[place(ids[0, j], where)]


def scenario_kernel(
    where, own_picked, other_picked, border_own, border_other, inverse_own, inverse_other,
    keep_ref, send_ref, picked, values,
):
    core, side = where[3], where[4]
    half_rows = border_own.shape[0]
    tiles = own_picked.shape[0]
    for j in range(tiles):
        picked[pl.ds(pl.multiple_of(j * TILE + core * HALF, HALF), HALF), :] = own_picked[j]
        picked[pl.ds(pl.multiple_of(j * TILE + (1 - core) * HALF, HALF), HALF), :] = other_picked[j]
    rows = lax.broadcasted_iota(jnp.int32, (half_rows, values.shape[1]), 0)
    own_start = pl.multiple_of(side * half_rows, half_rows)
    other_start = pl.multiple_of((1 - side) * half_rows, half_rows)
    live = where[5]

    def masked(product, start):
        return jnp.where(rows + start < live, product, 0.0).astype(BF16)

    whole = picked[...]
    values[pl.ds(own_start, half_rows), :] = masked(
        jnp.dot(border_own[...], whole, preferred_element_type=F32), own_start
    )
    values[pl.ds(other_start, half_rows), :] = masked(
        jnp.dot(border_other[...], whole, preferred_element_type=F32), other_start
    )
    operand = values[...]
    solved_own = masked(jnp.dot(inverse_own[...], operand, preferred_element_type=F32), own_start)
    solved_other = masked(jnp.dot(inverse_other[...], operand, preferred_element_type=F32), other_start)
    numbers = (((0,), (0,)), ((), ()))
    term = lax.dot_general(border_own[...], solved_own, numbers, preferred_element_type=F32)
    term += lax.dot_general(border_other[...], solved_other, numbers, preferred_element_type=F32)
    term = term.reshape(tiles, 2, HALF, term.shape[1])

    @pl.when(core == 0)
    def _():
        keep_ref[...] = term[:, 0]
        send_ref[...] = term[:, 1]

    @pl.when(core == 1)
    def _():
        keep_ref[...] = term[:, 1]
        send_ref[...] = term[:, 0]


def scatter_kernel(where, own_ids, other_ids, keep, arrived, out, total):
    both = ((own_ids, keep), (other_ids, arrived))
    spots = [[place(ids[0, j], where) for j in range(ids.shape[1])] for ids, _ in both]
    out[...] = jnp.zeros_like(out)
    for spot in spots[1]:
        total[spot] = jnp.zeros_like(total[spot])
    for j, spot in enumerate(spots[0]):
        total[spot] = keep[j]
    for j, spot in enumerate(spots[1]):
        total[spot] += arrived[j]
    for spot in spots[0] + spots[1]:
        out[spot] = total[spot].astype(BF16)


def update_kernel(where, start, precond, b1, b2, b3, *refs):
    pieces, (o0, o1, o2, o3, whole) = refs[:8], refs[8:]
    y, x, z, core = where[0], where[1], where[2], where[3]
    slots = (z, z ^ 1, 3 - z, (3 - z) ^ 1)
    for side in range(2):
        half = core if side == 0 else 1 - core
        for i in range(RING):
            piece = pieces[side * RING + i]
            base = ((x + i) % RING) * 4
            for j in range(RING):
                at = pl.multiple_of((base + slots[j]) * TILE + half * HALF, HALF)
                whole[pl.ds(at, HALF), :] = piece[j]
    operand = whole[...]
    span = operand.shape[0]
    own = precond[:, pl.ds(pl.multiple_of(y * span, span), span)]
    o0[...] = start[...] + jnp.dot(own, operand, preferred_element_type=F32)
    for block, out in ((b1, o1), (b2, o2), (b3, o3)):
        out[...] = jnp.dot(block[...], operand, preferred_element_type=F32)


def call(kernel, specs, outs, scratch=(), flops=0, moved=0):
    return pl.pallas_call(
        kernel,
        out_shape=outs,
        in_specs=specs,
        out_specs=jax.tree.map(lambda _: VMEM, outs),
        scratch_shapes=scratch,
        cost_estimate=pl.CostEstimate(flops=flops, bytes_accessed=moved, transcendentals=0),
        compiler_params=pltpu.CompilerParams(vmem_limit_bytes=32 * 1024 * 1024),
    )


def local(
    start_guess,
    right_side,
    root_diagonal,
    preconditioner,
    border_block,
    coupling_inverse,
    border_count,
    column_tiles,
):
    rows, cols = start_guess.shape
    shape = jax.ShapeDtypeStruct
    where = jnp.stack(
        [*(lax.axis_index(a).astype(jnp.int32) for a in (Y, X, Z, CORE, SIDE)), border_count[0]]
    )
    border, inverse = border_block[0], coupling_inverse[0]
    tiles = column_tiles.shape[1]
    everywhere = RING * RING * RING

    line = line_gather(start_guess.astype(BF16))
    span = preconditioner.shape[1] // RING

    def for_ahead(k):
        first = ((where[0] + k) % RING) * span
        return lax.dynamic_slice_in_dim(preconditioner, first, span, 1)

    block1 = to_ahead(for_ahead(1), Y, 1)
    line, block1, border_late, inverse_late, right_side = lax.optimization_barrier(
        (line, block1, border, inverse, right_side)
    )
    border_other = swap(border_late, SIDE)
    inverse_other = swap(inverse_late, SIDE)
    other_tiles = swap(column_tiles, CORE)
    copies = jnp.broadcast_to(line, (RING * RING, *line.shape))
    gathered = lax.all_to_all(copies, (Y, X), 0, 0, tiled=True)

    own_half, for_other = call(
        pick_kernel,
        [SMEM] * 3 + [VMEM],
        [shape((tiles, HALF, cols), BF16)] * 2,
    )(where, column_tiles, other_tiles, gathered.reshape(everywhere, HALF, cols))
    other_half = swap(for_other, CORE)
    keep, send = call(
        scenario_kernel,
        [SMEM] + [VMEM] * 6,
        [shape((tiles, HALF, cols), F32)] * 2,
        [pltpu.VMEM((tiles * TILE, cols), BF16), pltpu.VMEM((2 * border.shape[0], cols), BF16)],
    )(where, own_half, other_half, border, border_other, inverse, inverse_other)
    arrived = swap(send, CORE)
    spread = call(
        scatter_kernel,
        [SMEM] * 3 + [VMEM] * 2,
        shape((everywhere, HALF, cols), BF16),
        [pltpu.VMEM((everywhere, HALF, cols), F32)],
    )(where, column_tiles, other_tiles, keep, arrived)
    terms = lax.all_to_all(spread.reshape(RING * RING, RING, HALF, cols), (Y, X), 0, 0, tiled=True)
    line = terms.astype(F32).sum(axis=0)
    columns2, columns3, line = lax.optimization_barrier((for_ahead(2), for_ahead(3), line))
    block2, block3 = to_ahead(columns2, Y, 2), to_ahead(columns3, Y, 3)
    own_terms = right_side - root_diagonal[:, None] * start_guess
    line = line + jnp.concatenate([own_terms[None], jnp.zeros_like(line[1:])])
    met = pair(Z, line.astype(BF16), True).astype(F32)
    line = line + jnp.stack([met[1], met[0], met[3], met[2]])
    met = pair(Z, line.astype(BF16), False).astype(F32)
    line = line + jnp.concatenate([met[2:], met[:2]])

    mine = ring_pieces(line.astype(BF16), X)
    partners = [swap(piece, CORE) for piece in mine]
    parts = call(
        update_kernel,
        [SMEM] + [VMEM] * 13,
        [shape((rows, cols), F32)] * RING,
        [pltpu.VMEM((span, cols), BF16)],
    )(where, start_guess, preconditioner, block1, block2, block3, *mine, *partners)
    out = parts[0]
    for k in range(1, RING):
        out = out + from_ahead(parts[k], Y, k)
    return out


def solution(mesh):
    torus = Mesh(
        mesh.devices.reshape(RING, RING, RING, mesh.shape["rootr"], mesh.shape["rootc"]),
        (Y, X, Z, CORE, SIDE),
    )
    in_specs = (
        P(SCEN_ROOTR, SIDE),
        P(SCEN_ROOTR, SIDE),
        P(SCEN_ROOTR),
        P(SCEN_ROOTR, None),
        P(SCEN_ROOTR, SIDE, None),
        P(SCEN_ROOTR, SIDE, None),
        P(SCEN_ROOTR),
        P(SCEN_ROOTR, None),
    )
    return jax.shard_map(
        local, mesh=torus, in_specs=in_specs, out_specs=P(SCEN_ROOTR, SIDE), check_vma=False
    )
```

```python
import functools

import jax
import jax.numpy as jnp
from jax import lax
from jax.experimental import pallas as pl
from jax.experimental.pallas import tpu as pltpu
from jax.sharding import Mesh
from jax.sharding import PartitionSpec as P

TILE = 128
HALF = 64
RING = 4
Y, X, Z, CORE, SIDE = "scen_0", "scen_1", "scen_2", "rootr", "rootc"
SCEN_ROOTR = (Y, X, Z, CORE)
SWAP = [(0, 1), (1, 0)]
F32 = jnp.float32
BF16 = jnp.bfloat16

VMEM = pl.BlockSpec(memory_space=pltpu.VMEM)
SMEM = pl.BlockSpec(memory_space=pltpu.SMEM)


def swap(value, axis):
    return lax.ppermute(value, axis, SWAP)


def from_ahead(value, axis, distance):
    return lax.ppermute(value, axis, [(i, (i - distance) % RING) for i in range(RING)])


def to_ahead(value, axis, distance):
    return lax.ppermute(value, axis, [(i, (i + distance) % RING) for i in range(RING)])


def ring_pieces(value, axis):
    return [value] + [from_ahead(value, axis, k) for k in range(1, RING)]


def pair(axis, value, first):
    other = [1, 0, 3, 2] if first else [3, 2, 1, 0]
    return lax.ppermute(value, axis, list(enumerate(other)))


def line_gather(value):
    two = jnp.stack([value, pair(Z, value, True)])
    return jnp.concatenate([two, pair(Z, two, False)])


def line_slot(tile_z, z):
    return jnp.where(
        tile_z == z, 0, jnp.where(tile_z == (z ^ 1), 1, jnp.where(tile_z == 3 - z, 2, 3))
    )


def place(tile, where):
    return tile - tile % RING + line_slot(tile % RING, where[2])


def pick_kernel(where, own_ids, other_ids, gathered, own_ref, other_ref):
    for ids, out in ((other_ids, other_ref), (own_ids, own_ref)):
        for j in range(ids.shape[1]):
            out[j] = gathered[place(ids[0, j], where)]


def scenario_kernel(
    where, own_picked, other_picked, border_own, border_other, inverse_own, inverse_other,
    keep_ref, send_ref, picked, values,
):
    core, side = where[3], where[4]
    half_rows = border_own.shape[0]
    tiles = own_picked.shape[0]
    for j in range(tiles):
        picked[pl.ds(pl.multiple_of(j * TILE + core * HALF, HALF), HALF), :] = own_picked[j]
        picked[pl.ds(pl.multiple_of(j * TILE + (1 - core) * HALF, HALF), HALF), :] = other_picked[j]
    rows = lax.broadcasted_iota(jnp.int32, (half_rows, values.shape[1]), 0)
    own_start = pl.multiple_of(side * half_rows, half_rows)
    other_start = pl.multiple_of((1 - side) * half_rows, half_rows)
    live = where[5]

    def masked(product, start):
        return jnp.where(rows + start < live, product, 0.0).astype(BF16)

    whole = picked[...]
    values[pl.ds(own_start, half_rows), :] = masked(
        jnp.dot(border_own[...], whole, preferred_element_type=F32), own_start
    )
    values[pl.ds(other_start, half_rows), :] = masked(
        jnp.dot(border_other[...], whole, preferred_element_type=F32), other_start
    )
    operand = values[...]
    solved_own = masked(jnp.dot(inverse_own[...], operand, preferred_element_type=F32), own_start)
    solved_other = masked(jnp.dot(inverse_other[...], operand, preferred_element_type=F32), other_start)
    numbers = (((0,), (0,)), ((), ()))
    term = lax.dot_general(border_own[...], solved_own, numbers, preferred_element_type=F32)
    term += lax.dot_general(border_other[...], solved_other, numbers, preferred_element_type=F32)
    term = term.reshape(tiles, 2, HALF, term.shape[1])

    @pl.when(core == 0)
    def _():
        keep_ref[...] = term[:, 0]
        send_ref[...] = term[:, 1]

    @pl.when(core == 1)
    def _():
        keep_ref[...] = term[:, 1]
        send_ref[...] = term[:, 0]


def scatter_kernel(where, own_ids, other_ids, keep, arrived, out, total):
    both = ((own_ids, keep), (other_ids, arrived))
    spots = [[place(ids[0, j], where) for j in range(ids.shape[1])] for ids, _ in both]
    out[...] = jnp.zeros_like(out)
    for spot in spots[1]:
        total[spot] = jnp.zeros_like(total[spot])
    for j, spot in enumerate(spots[0]):
        total[spot] = keep[j]
    for j, spot in enumerate(spots[1]):
        total[spot] += arrived[j]
    for spot in spots[0] + spots[1]:
        out[spot] = total[spot].astype(BF16)


def update_kernel(where, start, precond, b1, b2, b3, *refs):
    pieces, (o0, o1, o2, o3, whole) = refs[:8], refs[8:]
    y, x, z, core = where[0], where[1], where[2], where[3]
    slots = (z, z ^ 1, 3 - z, (3 - z) ^ 1)
    for side in range(2):
        half = core if side == 0 else 1 - core
        for i in range(RING):
            piece = pieces[side * RING + i]
            base = ((x + i) % RING) * 4
            for j in range(RING):
                at = pl.multiple_of((base + slots[j]) * TILE + half * HALF, HALF)
                whole[pl.ds(at, HALF), :] = piece[j]
    operand = whole[...]
    span = operand.shape[0]
    own = precond[:, pl.ds(pl.multiple_of(y * span, span), span)]
    o0[...] = start[...] + jnp.dot(own, operand, preferred_element_type=F32)
    for block, out in ((b1, o1), (b2, o2), (b3, o3)):
        out[...] = jnp.dot(block[...], operand, preferred_element_type=F32)


def call(kernel, specs, outs, scratch=(), flops=0, moved=0):
    return pl.pallas_call(
        kernel,
        out_shape=outs,
        in_specs=specs,
        out_specs=jax.tree.map(lambda _: VMEM, outs),
        scratch_shapes=scratch,
        cost_estimate=pl.CostEstimate(flops=flops, bytes_accessed=moved, transcendentals=0),
        compiler_params=pltpu.CompilerParams(vmem_limit_bytes=32 * 1024 * 1024),
    )


def local(
    start_guess,
    right_side,
    root_diagonal,
    preconditioner,
    border_block,
    coupling_inverse,
    border_count,
    column_tiles,
):
    rows, cols = start_guess.shape
    shape = jax.ShapeDtypeStruct
    where = jnp.stack(
        [*(lax.axis_index(a).astype(jnp.int32) for a in (Y, X, Z, CORE, SIDE)), border_count[0]]
    )
    border, inverse = border_block[0], coupling_inverse[0]
    tiles = column_tiles.shape[1]
    everywhere = RING * RING * RING

    line = line_gather(start_guess.astype(BF16))
    span = preconditioner.shape[1] // RING

    def for_ahead(k):
        first = ((where[0] + k) % RING) * span
        return lax.dynamic_slice_in_dim(preconditioner, first, span, 1)

    block1 = to_ahead(for_ahead(1), Y, 1)
    line, block1, border_late, inverse_late = lax.optimization_barrier((line, block1, border, inverse))
    border_other = swap(border_late, SIDE)
    inverse_other = swap(inverse_late, SIDE)
    other_tiles = swap(column_tiles, CORE)
    copies = jnp.broadcast_to(line, (RING * RING, *line.shape))
    gathered = lax.all_to_all(copies, (Y, X), 0, 0, tiled=True)

    own_half, for_other = call(
        pick_kernel,
        [SMEM] * 3 + [VMEM],
        [shape((tiles, HALF, cols), BF16)] * 2,
    )(where, column_tiles, other_tiles, gathered.reshape(everywhere, HALF, cols))
    other_half = swap(for_other, CORE)
    keep, send = call(
        scenario_kernel,
        [SMEM] + [VMEM] * 6,
        [shape((tiles, HALF, cols), F32)] * 2,
        [pltpu.VMEM((tiles * TILE, cols), BF16), pltpu.VMEM((2 * border.shape[0], cols), BF16)],
    )(where, own_half, other_half, border, border_other, inverse, inverse_other)
    arrived = swap(send, CORE)
    spread = call(
        scatter_kernel,
        [SMEM] * 3 + [VMEM] * 2,
        shape((everywhere, HALF, cols), BF16),
        [pltpu.VMEM((everywhere, HALF, cols), F32)],
    )(where, column_tiles, other_tiles, keep, arrived)
    terms = lax.all_to_all(spread.reshape(RING * RING, RING, HALF, cols), (Y, X), 0, 0, tiled=True)
    line = terms.astype(F32).sum(axis=0)
    columns2, columns3, line = lax.optimization_barrier((for_ahead(2), for_ahead(3), line))
    block2, block3 = to_ahead(columns2, Y, 2), to_ahead(columns3, Y, 3)
    own_terms = right_side - root_diagonal[:, None] * start_guess
    line = line + jnp.concatenate([own_terms[None], jnp.zeros_like(line[1:])])
    met = pair(Z, line.astype(BF16), True).astype(F32)
    line = line + jnp.stack([met[1], met[0], met[3], met[2]])
    met = pair(Z, line.astype(BF16), False).astype(F32)
    line = line + jnp.concatenate([met[2:], met[:2]])

    mine = ring_pieces(line.astype(BF16), X)
    partners = [swap(piece, CORE) for piece in mine]
    parts = call(
        update_kernel,
        [SMEM] + [VMEM] * 13,
        [shape((rows, cols), F32)] * RING,
        [pltpu.VMEM((span, cols), BF16)],
    )(where, start_guess, preconditioner, block1, block2, block3, *mine, *partners)
    out = parts[0]
    for k in range(1, RING):
        out = out + from_ahead(parts[k], Y, k)
    return out


def solution(mesh):
    torus = Mesh(
        mesh.devices.reshape(RING, RING, RING, mesh.shape["rootr"], mesh.shape["rootc"]),
        (Y, X, Z, CORE, SIDE),
    )
    in_specs = (
        P(SCEN_ROOTR, SIDE),
        P(SCEN_ROOTR, SIDE),
        P(SCEN_ROOTR),
        P(SCEN_ROOTR, None),
        P(SCEN_ROOTR, SIDE, None),
        P(SCEN_ROOTR, SIDE, None),
        P(SCEN_ROOTR),
        P(SCEN_ROOTR, None),
    )
    return jax.shard_map(
        local, mesh=torus, in_specs=in_specs, out_specs=P(SCEN_ROOTR, SIDE), check_vma=False
    )
```

```python
import functools

import jax
import jax.numpy as jnp
from jax import lax
from jax.experimental import pallas as pl
from jax.experimental.pallas import tpu as pltpu
from jax.sharding import Mesh
from jax.sharding import PartitionSpec as P

TILE = 128
HALF = 64
RING = 4
Y, X, Z, CORE, SIDE = "scen_0", "scen_1", "scen_2", "rootr", "rootc"
SCEN_ROOTR = (Y, X, Z, CORE)
SWAP = [(0, 1), (1, 0)]
F32 = jnp.float32
BF16 = jnp.bfloat16

VMEM = pl.BlockSpec(memory_space=pltpu.VMEM)
SMEM = pl.BlockSpec(memory_space=pltpu.SMEM)


def swap(value, axis):
    return lax.ppermute(value, axis, SWAP)


def from_ahead(value, axis, distance):
    return lax.ppermute(value, axis, [(i, (i - distance) % RING) for i in range(RING)])


def to_ahead(value, axis, distance):
    return lax.ppermute(value, axis, [(i, (i + distance) % RING) for i in range(RING)])


def ring_pieces(value, axis):
    return [value] + [from_ahead(value, axis, k) for k in range(1, RING)]


def across(value, distance, turn):
    pairs = []
    for y in range(RING):
        for x in range(RING):
            for core in range(2):
                if core == turn:
                    there = ((y + distance) % RING, x)
                else:
                    there = (y, (x + distance) % RING)
                pairs.append(((y * RING + x) * 2 + core, (there[0] * RING + there[1]) * 2 + core))
    return lax.ppermute(value, (Y, X, CORE), pairs)


def pair(axis, value, first):
    other = [1, 0, 3, 2] if first else [3, 2, 1, 0]
    return lax.ppermute(value, axis, list(enumerate(other)))


def line_gather(value):
    two = jnp.stack([value, pair(Z, value, True)])
    return jnp.concatenate([two, pair(Z, two, False)])


def line_slot(tile_z, z):
    return jnp.where(
        tile_z == z, 0, jnp.where(tile_z == (z ^ 1), 1, jnp.where(tile_z == 3 - z, 2, 3))
    )


def place(tile, where):
    return tile - tile % RING + line_slot(tile % RING, where[2])


def pick_kernel(where, own_ids, other_ids, gathered, own_ref, other_ref):
    for ids, out in ((other_ids, other_ref), (own_ids, own_ref)):
        for j in range(ids.shape[1]):
            out[j] = gathered[place(ids[0, j], where)]


def scenario_kernel(
    where, own_picked, other_picked, border_own, border_other, inverse_own, inverse_other,
    keep_ref, send_ref, picked, values,
):
    core, side = where[3], where[4]
    half_rows = border_own.shape[0]
    tiles = own_picked.shape[0]
    for j in range(tiles):
        picked[pl.ds(pl.multiple_of(j * TILE + core * HALF, HALF), HALF), :] = own_picked[j]
        picked[pl.ds(pl.multiple_of(j * TILE + (1 - core) * HALF, HALF), HALF), :] = other_picked[j]
    rows = lax.broadcasted_iota(jnp.int32, (half_rows, values.shape[1]), 0)
    own_start = pl.multiple_of(side * half_rows, half_rows)
    other_start = pl.multiple_of((1 - side) * half_rows, half_rows)
    live = where[5]

    def masked(product, start):
        return jnp.where(rows + start < live, product, 0.0).astype(BF16)

    whole = picked[...]
    values[pl.ds(own_start, half_rows), :] = masked(
        jnp.dot(border_own[...], whole, preferred_element_type=F32), own_start
    )
    values[pl.ds(other_start, half_rows), :] = masked(
        jnp.dot(border_other[...], whole, preferred_element_type=F32), other_start
    )
    operand = values[...]
    solved_own = masked(jnp.dot(inverse_own[...], operand, preferred_element_type=F32), own_start)
    solved_other = masked(jnp.dot(inverse_other[...], operand, preferred_element_type=F32), other_start)
    numbers = (((0,), (0,)), ((), ()))
    term = lax.dot_general(border_own[...], solved_own, numbers, preferred_element_type=F32)
    term += lax.dot_general(border_other[...], solved_other, numbers, preferred_element_type=F32)
    term = term.reshape(tiles, 2, HALF, term.shape[1])

    @pl.when(core == 0)
    def _():
        keep_ref[...] = term[:, 0]
        send_ref[...] = term[:, 1]

    @pl.when(core == 1)
    def _():
        keep_ref[...] = term[:, 1]
        send_ref[...] = term[:, 0]


def spread_place(tile, where):
    dy = (tile // 16 - where[0] + RING) % RING
    dx = ((tile // RING) % RING - where[1] + RING) % RING
    slot = line_slot(tile % RING, where[2])
    first = where[3] == 0
    return jnp.where(first, dy, dx), jnp.where(first, dx, dy) * RING + slot


def scatter_kernel(where, own_ids, other_ids, keep, arrived, near, c1, c2, c3, total):
    spots = []
    for ids in (own_ids, other_ids):
        for j in range(ids.shape[1]):
            chunk, rest = spread_place(ids[0, j], where)
            spots.append((chunk, rest, chunk * 16 + rest))
    half = len(spots) // 2
    near_rows = near.shape[0]
    total[0:near_rows] = jnp.zeros_like(near)
    chunks = (c1, c2, c3)
    for chunk in chunks:
        chunk[...] = jnp.zeros_like(chunk)
    for _, _, spot in spots[half:]:
        total[spot] = jnp.zeros_like(total[spot])
    for j, (_, _, spot) in enumerate(spots[:half]):
        total[spot] = keep[j]
    for j, (_, _, spot) in enumerate(spots[half:]):
        total[spot] += arrived[j]
    near[...] = total[0:near_rows]
    for chunk, rest, spot in spots:
        for k, out in enumerate(chunks):

            @pl.when(chunk == k + 1)
            def _():
                out[rest] = total[spot].astype(BF16)


def update_kernel(where, start, precond, b1, b2, b3, *refs):
    pieces, (o0, o1, o2, o3, whole) = refs[:8], refs[8:]
    y, x, z, core = where[0], where[1], where[2], where[3]
    slots = (z, z ^ 1, 3 - z, (3 - z) ^ 1)
    for side in range(2):
        half = core if side == 0 else 1 - core
        for i in range(RING):
            piece = pieces[side * RING + i]
            base = ((x + i) % RING) * 4
            for j in range(RING):
                at = pl.multiple_of((base + slots[j]) * TILE + half * HALF, HALF)
                whole[pl.ds(at, HALF), :] = piece[j]
    operand = whole[...]
    span = operand.shape[0]
    own = precond[:, pl.ds(pl.multiple_of(y * span, span), span)]
    o0[...] = start[...] + jnp.dot(own, operand, preferred_element_type=F32)
    for block, out in ((b1, o1), (b2, o2), (b3, o3)):
        out[...] = jnp.dot(block[...], operand, preferred_element_type=F32)


def call(kernel, specs, outs, scratch=(), flops=0, moved=0):
    return pl.pallas_call(
        kernel,
        out_shape=outs,
        in_specs=specs,
        out_specs=jax.tree.map(lambda _: VMEM, outs),
        scratch_shapes=scratch,
        cost_estimate=pl.CostEstimate(flops=flops, bytes_accessed=moved, transcendentals=0),
        compiler_params=pltpu.CompilerParams(vmem_limit_bytes=32 * 1024 * 1024),
    )


def local(
    start_guess,
    right_side,
    root_diagonal,
    preconditioner,
    border_block,
    coupling_inverse,
    border_count,
    column_tiles,
):
    rows, cols = start_guess.shape
    shape = jax.ShapeDtypeStruct
    where = jnp.stack(
        [*(lax.axis_index(a).astype(jnp.int32) for a in (Y, X, Z, CORE, SIDE)), border_count[0]]
    )
    border, inverse = border_block[0], coupling_inverse[0]
    tiles = column_tiles.shape[1]
    everywhere = RING * RING * RING

    line = line_gather(start_guess.astype(BF16))
    span = preconditioner.shape[1] // RING

    def for_ahead(k):
        first = ((where[0] + k) % RING) * span
        return lax.dynamic_slice_in_dim(preconditioner, first, span, 1)

    block1 = to_ahead(for_ahead(1), Y, 1)
    line, block1, border_late, inverse_late = lax.optimization_barrier((line, block1, border, inverse))
    border_other = swap(border_late, SIDE)
    inverse_other = swap(inverse_late, SIDE)
    other_tiles = swap(column_tiles, CORE)
    copies = jnp.broadcast_to(line, (RING * RING, *line.shape))
    gathered = lax.all_to_all(copies, (Y, X), 0, 0, tiled=True)

    own_half, for_other = call(
        pick_kernel,
        [SMEM] * 3 + [VMEM],
        [shape((tiles, HALF, cols), BF16)] * 2,
    )(where, column_tiles, other_tiles, gathered.reshape(everywhere, HALF, cols))
    other_half = swap(for_other, CORE)
    keep, send = call(
        scenario_kernel,
        [SMEM] + [VMEM] * 6,
        [shape((tiles, HALF, cols), F32)] * 2,
        [pltpu.VMEM((tiles * TILE, cols), BF16), pltpu.VMEM((2 * border.shape[0], cols), BF16)],
    )(where, own_half, other_half, border, border_other, inverse, inverse_other)
    arrived = swap(send, CORE)
    near_tiles = RING * RING
    near_shape = (near_tiles, HALF, cols)
    near, *chunks = call(
        scatter_kernel,
        [SMEM] * 3 + [VMEM] * 2,
        [shape(near_shape, F32)] + [shape(near_shape, BF16)] * (RING - 1),
        [pltpu.VMEM((everywhere, HALF, cols), F32)],
    )(where, column_tiles, other_tiles, keep, arrived)
    plane = near
    for k, chunk in enumerate(chunks):
        plane = plane + across(chunk, k + 1, 0).astype(F32)
    plane = plane.reshape(RING, RING, HALF, cols)
    line = plane[0]
    for k in range(1, RING):
        line = line + across(plane[k].astype(BF16), k, 1).astype(F32)
    columns2, columns3, line = lax.optimization_barrier((for_ahead(2), for_ahead(3), line))
    block2, block3 = to_ahead(columns2, Y, 2), to_ahead(columns3, Y, 3)
    own_terms = right_side - root_diagonal[:, None] * start_guess
    line = line + jnp.concatenate([own_terms[None], jnp.zeros_like(line[1:])])
    met = pair(Z, line.astype(BF16), True).astype(F32)
    line = line + jnp.stack([met[1], met[0], met[3], met[2]])
    met = pair(Z, line.astype(BF16), False).astype(F32)
    line = line + jnp.concatenate([met[2:], met[:2]])

    mine = ring_pieces(line.astype(BF16), X)
    partners = [swap(piece, CORE) for piece in mine]
    parts = call(
        update_kernel,
        [SMEM] + [VMEM] * 13,
        [shape((rows, cols), F32)] * RING,
        [pltpu.VMEM((span, cols), BF16)],
    )(where, start_guess, preconditioner, block1, block2, block3, *mine, *partners)
    out = parts[0]
    for k in range(1, RING):
        out = out + from_ahead(parts[k], Y, k)
    return out


def solution(mesh):
    torus = Mesh(
        mesh.devices.reshape(RING, RING, RING, mesh.shape["rootr"], mesh.shape["rootc"]),
        (Y, X, Z, CORE, SIDE),
    )
    in_specs = (
        P(SCEN_ROOTR, SIDE),
        P(SCEN_ROOTR, SIDE),
        P(SCEN_ROOTR),
        P(SCEN_ROOTR, None),
        P(SCEN_ROOTR, SIDE, None),
        P(SCEN_ROOTR, SIDE, None),
        P(SCEN_ROOTR),
        P(SCEN_ROOTR, None),
    )
    return jax.shard_map(
        local, mesh=torus, in_specs=in_specs, out_specs=P(SCEN_ROOTR, SIDE), check_vma=False
    )
```

```python
import functools

import jax
import jax.numpy as jnp
from jax import lax
from jax.experimental import pallas as pl
from jax.experimental.pallas import tpu as pltpu
from jax.sharding import Mesh
from jax.sharding import PartitionSpec as P

TILE = 128
HALF = 64
RING = 4
Y, X, Z, CORE, SIDE = "scen_0", "scen_1", "scen_2", "rootr", "rootc"
SCEN_ROOTR = (Y, X, Z, CORE)
SWAP = [(0, 1), (1, 0)]
F32 = jnp.float32
BF16 = jnp.bfloat16

VMEM = pl.BlockSpec(memory_space=pltpu.VMEM)
SMEM = pl.BlockSpec(memory_space=pltpu.SMEM)


def swap(value, axis):
    return lax.ppermute(value, axis, SWAP)


def from_ahead(value, axis, distance):
    return lax.ppermute(value, axis, [(i, (i - distance) % RING) for i in range(RING)])


def to_ahead(value, axis, distance):
    return lax.ppermute(value, axis, [(i, (i + distance) % RING) for i in range(RING)])


def ring_pieces(value, axis):
    return [value] + [from_ahead(value, axis, k) for k in range(1, RING)]


def across(value, distance, turn):
    pairs = []
    for y in range(RING):
        for x in range(RING):
            for core in range(2):
                if core == turn:
                    there = ((y + distance) % RING, x)
                else:
                    there = (y, (x + distance) % RING)
                pairs.append(((y * RING + x) * 2 + core, (there[0] * RING + there[1]) * 2 + core))
    return lax.ppermute(value, (Y, X, CORE), pairs)


def pair(axis, value, first):
    other = [1, 0, 3, 2] if first else [3, 2, 1, 0]
    return lax.ppermute(value, axis, list(enumerate(other)))


def line_gather(value):
    two = jnp.stack([value, pair(Z, value, True)])
    return jnp.concatenate([two, pair(Z, two, False)])


def line_slot(tile_z, z):
    return jnp.where(
        tile_z == z, 0, jnp.where(tile_z == (z ^ 1), 1, jnp.where(tile_z == 3 - z, 2, 3))
    )


def spread_place(tile, where):
    dy = (tile // 16 - where[0] + RING) % RING
    dx = ((tile // RING) % RING - where[1] + RING) % RING
    slot = line_slot(tile % RING, where[2])
    first = where[3] == 0
    return jnp.where(first, dy, dx), jnp.where(first, dx, dy) * RING + slot


def pick_kernel(where, own_ids, other_ids, p0, p1, p2, p3, own_ref, other_ref):
    for ids, out in ((other_ids, other_ref), (own_ids, own_ref)):
        for j in range(ids.shape[1]):
            chunk, rest = spread_place(ids[0, j], where)
            for k, piece in enumerate((p0, p1, p2, p3)):

                @pl.when(chunk == k)
                def _():
                    out[j] = piece[rest]


def scenario_kernel(
    where, own_picked, other_picked, border_own, border_other, inverse_own, inverse_other,
    keep_ref, send_ref, picked, values,
):
    core, side = where[3], where[4]
    half_rows = border_own.shape[0]
    tiles = own_picked.shape[0]
    for j in range(tiles):
        picked[pl.ds(pl.multiple_of(j * TILE + core * HALF, HALF), HALF), :] = own_picked[j]
        picked[pl.ds(pl.multiple_of(j * TILE + (1 - core) * HALF, HALF), HALF), :] = other_picked[j]
    rows = lax.broadcasted_iota(jnp.int32, (half_rows, values.shape[1]), 0)
    own_start = pl.multiple_of(side * half_rows, half_rows)
    other_start = pl.multiple_of((1 - side) * half_rows, half_rows)
    live = where[5]

    def masked(product, start):
        return jnp.where(rows + start < live, product, 0.0).astype(BF16)

    whole = picked[...]
    values[pl.ds(own_start, half_rows), :] = masked(
        jnp.dot(border_own[...], whole, preferred_element_type=F32), own_start
    )
    values[pl.ds(other_start, half_rows), :] = masked(
        jnp.dot(border_other[...], whole, preferred_element_type=F32), other_start
    )
    operand = values[...]
    solved_own = masked(jnp.dot(inverse_own[...], operand, preferred_element_type=F32), own_start)
    solved_other = masked(jnp.dot(inverse_other[...], operand, preferred_element_type=F32), other_start)
    numbers = (((0,), (0,)), ((), ()))
    term = lax.dot_general(border_own[...], solved_own, numbers, preferred_element_type=F32)
    term += lax.dot_general(border_other[...], solved_other, numbers, preferred_element_type=F32)
    term = term.reshape(tiles, 2, HALF, term.shape[1])

    @pl.when(core == 0)
    def _():
        keep_ref[...] = term[:, 0]
        send_ref[...] = term[:, 1]

    @pl.when(core == 1)
    def _():
        keep_ref[...] = term[:, 1]
        send_ref[...] = term[:, 0]


def scatter_kernel(where, own_ids, other_ids, keep, arrived, near, c1, c2, c3, total):
    spots = []
    for ids in (own_ids, other_ids):
        for j in range(ids.shape[1]):
            chunk, rest = spread_place(ids[0, j], where)
            spots.append((chunk, rest, chunk * 16 + rest))
    half = len(spots) // 2
    near_rows = near.shape[0]
    total[0:near_rows] = jnp.zeros_like(near)
    chunks = (c1, c2, c3)
    for chunk in chunks:
        chunk[...] = jnp.zeros_like(chunk)
    for _, _, spot in spots[half:]:
        total[spot] = jnp.zeros_like(total[spot])
    for j, (_, _, spot) in enumerate(spots[:half]):
        total[spot] = keep[j]
    for j, (_, _, spot) in enumerate(spots[half:]):
        total[spot] += arrived[j]
    near[...] = total[0:near_rows]
    for chunk, rest, spot in spots:
        for k, out in enumerate(chunks):

            @pl.when(chunk == k + 1)
            def _():
                out[rest] = total[spot].astype(BF16)


def update_kernel(where, start, precond, b1, b2, b3, *refs):
    pieces, (o0, o1, o2, o3, whole) = refs[:8], refs[8:]
    y, x, z, core = where[0], where[1], where[2], where[3]
    slots = (z, z ^ 1, 3 - z, (3 - z) ^ 1)
    for side in range(2):
        half = core if side == 0 else 1 - core
        for i in range(RING):
            piece = pieces[side * RING + i]
            base = ((x + i) % RING) * 4
            for j in range(RING):
                at = pl.multiple_of((base + slots[j]) * TILE + half * HALF, HALF)
                whole[pl.ds(at, HALF), :] = piece[j]
    operand = whole[...]
    span = operand.shape[0]
    own = precond[:, pl.ds(pl.multiple_of(y * span, span), span)]
    o0[...] = start[...] + jnp.dot(own, operand, preferred_element_type=F32)
    for block, out in ((b1, o1), (b2, o2), (b3, o3)):
        out[...] = jnp.dot(block[...], operand, preferred_element_type=F32)


def call(kernel, specs, outs, scratch=(), flops=0, moved=0):
    return pl.pallas_call(
        kernel,
        out_shape=outs,
        in_specs=specs,
        out_specs=jax.tree.map(lambda _: VMEM, outs),
        scratch_shapes=scratch,
        cost_estimate=pl.CostEstimate(flops=flops, bytes_accessed=moved, transcendentals=0),
        compiler_params=pltpu.CompilerParams(vmem_limit_bytes=32 * 1024 * 1024),
    )


def local(
    start_guess,
    right_side,
    root_diagonal,
    preconditioner,
    border_block,
    coupling_inverse,
    border_count,
    column_tiles,
):
    rows, cols = start_guess.shape
    shape = jax.ShapeDtypeStruct
    where = jnp.stack(
        [*(lax.axis_index(a).astype(jnp.int32) for a in (Y, X, Z, CORE, SIDE)), border_count[0]]
    )
    border, inverse = border_block[0], coupling_inverse[0]
    tiles = column_tiles.shape[1]
    everywhere = RING * RING * RING

    line = line_gather(start_guess.astype(BF16))
    span = preconditioner.shape[1] // RING

    def for_ahead(k):
        first = ((where[0] + k) % RING) * span
        return lax.dynamic_slice_in_dim(preconditioner, first, span, 1)

    block1 = to_ahead(for_ahead(1), Y, 1)
    other_tiles = swap(column_tiles, CORE)
    line, block1, other_tiles, border_late, inverse_late = lax.optimization_barrier(
        (line, block1, other_tiles, border, inverse)
    )
    border_other = swap(border_late, SIDE)
    inverse_other = swap(inverse_late, SIDE)
    plane = jnp.concatenate([line] + [across(line, -k, 1) for k in range(1, RING)])
    gathered = [plane] + [across(plane, -k, 0) for k in range(1, RING)]

    own_half, for_other = call(
        pick_kernel,
        [SMEM] * 3 + [VMEM] * 4,
        [shape((tiles, HALF, cols), BF16)] * 2,
    )(where, column_tiles, other_tiles, *gathered)
    other_half = swap(for_other, CORE)
    keep, send = call(
        scenario_kernel,
        [SMEM] + [VMEM] * 6,
        [shape((tiles, HALF, cols), F32)] * 2,
        [pltpu.VMEM((tiles * TILE, cols), BF16), pltpu.VMEM((2 * border.shape[0], cols), BF16)],
    )(where, own_half, other_half, border, border_other, inverse, inverse_other)
    arrived = swap(send, CORE)
    near_tiles = RING * RING
    near_shape = (near_tiles, HALF, cols)
    near, *chunks = call(
        scatter_kernel,
        [SMEM] * 3 + [VMEM] * 2,
        [shape(near_shape, F32)] + [shape(near_shape, BF16)] * (RING - 1),
        [pltpu.VMEM((everywhere, HALF, cols), F32)],
    )(where, column_tiles, other_tiles, keep, arrived)
    plane = near
    for k, chunk in enumerate(chunks):
        plane = plane + across(chunk, k + 1, 0).astype(F32)
    plane = plane.reshape(RING, RING, HALF, cols)
    line = plane[0]
    for k in range(1, RING):
        line = line + across(plane[k].astype(BF16), k, 1).astype(F32)
    columns2, columns3, line = lax.optimization_barrier((for_ahead(2), for_ahead(3), line))
    block2, block3 = to_ahead(columns2, Y, 2), to_ahead(columns3, Y, 3)
    own_terms = right_side - root_diagonal[:, None] * start_guess
    line = line + jnp.concatenate([own_terms[None], jnp.zeros_like(line[1:])])
    met = pair(Z, line.astype(BF16), True).astype(F32)
    line = line + jnp.stack([met[1], met[0], met[3], met[2]])
    met = pair(Z, line.astype(BF16), False).astype(F32)
    line = line + jnp.concatenate([met[2:], met[:2]])

    mine = ring_pieces(line.astype(BF16), X)
    partners = [swap(piece, CORE) for piece in mine]
    parts = call(
        update_kernel,
        [SMEM] + [VMEM] * 13,
        [shape((rows, cols), F32)] * RING,
        [pltpu.VMEM((span, cols), BF16)],
    )(where, start_guess, preconditioner, block1, block2, block3, *mine, *partners)
    out = parts[0]
    for k in range(1, RING):
        out = out + from_ahead(parts[k], Y, k)
    return out


def solution(mesh):
    torus = Mesh(
        mesh.devices.reshape(RING, RING, RING, mesh.shape["rootr"], mesh.shape["rootc"]),
        (Y, X, Z, CORE, SIDE),
    )
    in_specs = (
        P(SCEN_ROOTR, SIDE),
        P(SCEN_ROOTR, SIDE),
        P(SCEN_ROOTR),
        P(SCEN_ROOTR, None),
        P(SCEN_ROOTR, SIDE, None),
        P(SCEN_ROOTR, SIDE, None),
        P(SCEN_ROOTR),
        P(SCEN_ROOTR, None),
    )
    return jax.shard_map(
        local, mesh=torus, in_specs=in_specs, out_specs=P(SCEN_ROOTR, SIDE), check_vma=False
    )
```

```python
import functools

import jax
import jax.numpy as jnp
from jax import lax
from jax.experimental import pallas as pl
from jax.experimental.pallas import tpu as pltpu
from jax.sharding import Mesh
from jax.sharding import PartitionSpec as P

TILE = 128
HALF = 64
RING = 4
Y, X, Z, CORE, SIDE = "scen_0", "scen_1", "scen_2", "rootr", "rootc"
SCEN_ROOTR = (Y, X, Z, CORE)
SWAP = [(0, 1), (1, 0)]
F32 = jnp.float32
BF16 = jnp.bfloat16

VMEM = pl.BlockSpec(memory_space=pltpu.VMEM)
SMEM = pl.BlockSpec(memory_space=pltpu.SMEM)


def swap(value, axis):
    return lax.ppermute(value, axis, SWAP)


def from_ahead(value, axis, distance):
    return lax.ppermute(value, axis, [(i, (i - distance) % RING) for i in range(RING)])


def to_ahead(value, axis, distance):
    return lax.ppermute(value, axis, [(i, (i + distance) % RING) for i in range(RING)])


def ring_pieces(value, axis):
    return [value] + [from_ahead(value, axis, k) for k in range(1, RING)]


def across(value, distance, turn):
    pairs = []
    for y in range(RING):
        for x in range(RING):
            for core in range(2):
                if core == turn:
                    there = ((y + distance) % RING, x)
                else:
                    there = (y, (x + distance) % RING)
                pairs.append(((y * RING + x) * 2 + core, (there[0] * RING + there[1]) * 2 + core))
    return lax.ppermute(value, (Y, X, CORE), pairs)


def pair(axis, value, first):
    other = [1, 0, 3, 2] if first else [3, 2, 1, 0]
    return lax.ppermute(value, axis, list(enumerate(other)))


def line_gather(value):
    two = jnp.stack([value, pair(Z, value, True)])
    return jnp.concatenate([two, pair(Z, two, False)])


def line_slot(tile_z, z):
    return jnp.where(
        tile_z == z, 0, jnp.where(tile_z == (z ^ 1), 1, jnp.where(tile_z == 3 - z, 2, 3))
    )


def spread_place(tile, where):
    dy = (tile // 16 - where[0] + RING) % RING
    dx = ((tile // RING) % RING - where[1] + RING) % RING
    slot = line_slot(tile % RING, where[2])
    first = where[3] == 0
    return jnp.where(first, dy, dx), jnp.where(first, dx, dy) * RING + slot


def pick_kernel(where, own_ids, other_ids, p0, p1, p2, p3, own_ref, other_ref):
    for ids, out in ((other_ids, other_ref), (own_ids, own_ref)):
        for j in range(ids.shape[1]):
            chunk, rest = spread_place(ids[0, j], where)
            value = p0[rest]
            for k, piece in enumerate((p1, p2, p3)):
                value = jnp.where(chunk == k + 1, piece[rest], value)
            out[j] = value


def scenario_kernel(
    where, own_picked, other_picked, border_own, border_other, inverse_own, inverse_other,
    keep_ref, send_ref, picked, values,
):
    core, side = where[3], where[4]
    half_rows = border_own.shape[0]
    tiles = own_picked.shape[0]
    for j in range(tiles):
        picked[pl.ds(pl.multiple_of(j * TILE + core * HALF, HALF), HALF), :] = own_picked[j]
        picked[pl.ds(pl.multiple_of(j * TILE + (1 - core) * HALF, HALF), HALF), :] = other_picked[j]
    rows = lax.broadcasted_iota(jnp.int32, (half_rows, values.shape[1]), 0)
    own_start = pl.multiple_of(side * half_rows, half_rows)
    other_start = pl.multiple_of((1 - side) * half_rows, half_rows)
    live = where[5]

    def masked(product, start):
        return jnp.where(rows + start < live, product, 0.0).astype(BF16)

    whole = picked[...]
    values[pl.ds(own_start, half_rows), :] = masked(
        jnp.dot(border_own[...], whole, preferred_element_type=F32), own_start
    )
    values[pl.ds(other_start, half_rows), :] = masked(
        jnp.dot(border_other[...], whole, preferred_element_type=F32), other_start
    )
    operand = values[...]
    solved_own = masked(jnp.dot(inverse_own[...], operand, preferred_element_type=F32), own_start)
    solved_other = masked(jnp.dot(inverse_other[...], operand, preferred_element_type=F32), other_start)
    numbers = (((0,), (0,)), ((), ()))
    turned = lax.dot_general(solved_own, border_own[...], numbers, preferred_element_type=F32)
    turned += lax.dot_general(solved_other, border_other[...], numbers, preferred_element_type=F32)
    term = turned.T.reshape(tiles, 2, HALF, turned.shape[0])

    @pl.when(core == 0)
    def _():
        keep_ref[...] = term[:, 0]
        send_ref[...] = term[:, 1]

    @pl.when(core == 1)
    def _():
        keep_ref[...] = term[:, 1]
        send_ref[...] = term[:, 0]


def scatter_kernel(where, own_ids, other_ids, keep, arrived, near, c1, c2, c3, total):
    spots = []
    for ids in (own_ids, other_ids):
        for j in range(ids.shape[1]):
            chunk, rest = spread_place(ids[0, j], where)
            spots.append((chunk, rest, chunk * 16 + rest))
    half = len(spots) // 2
    outs = (near, c1, c2, c3)
    for out in outs:
        out[...] = jnp.zeros_like(out)
    for _, _, spot in spots[half:]:
        total[spot] = jnp.zeros_like(total[spot])
    for j, (_, _, spot) in enumerate(spots[:half]):
        total[spot] = keep[j]
    for j, (_, _, spot) in enumerate(spots[half:]):
        total[spot] += arrived[j]
    for chunk, rest, spot in spots:
        value = total[spot]
        for k, out in enumerate(outs):
            out[rest] = jnp.where(chunk == k, value.astype(out.dtype), out[rest])


def update_kernel(where, start, precond, b1, b2, b3, *refs):
    pieces, (o0, o1, o2, o3, whole) = refs[:8], refs[8:]
    y, x, z, core = where[0], where[1], where[2], where[3]
    slots = (z, z ^ 1, 3 - z, (3 - z) ^ 1)
    for side in range(2):
        half = core if side == 0 else 1 - core
        for i in range(RING):
            piece = pieces[side * RING + i]
            base = ((x + i) % RING) * 4
            for j in range(RING):
                at = pl.multiple_of((base + slots[j]) * TILE + half * HALF, HALF)
                whole[pl.ds(at, HALF), :] = piece[j]
    operand = whole[...]
    span = operand.shape[0]
    own = precond[:, pl.ds(pl.multiple_of(y * span, span), span)]
    o0[...] = start[...] + jnp.dot(own, operand, preferred_element_type=F32)
    for block, out in ((b1, o1), (b2, o2), (b3, o3)):
        out[...] = jnp.dot(block[...], operand, preferred_element_type=F32)


def call(kernel, specs, outs, scratch=(), flops=0, moved=0):
    return pl.pallas_call(
        kernel,
        out_shape=outs,
        in_specs=specs,
        out_specs=jax.tree.map(lambda _: VMEM, outs),
        scratch_shapes=scratch,
        cost_estimate=pl.CostEstimate(flops=flops, bytes_accessed=moved, transcendentals=0),
        compiler_params=pltpu.CompilerParams(vmem_limit_bytes=32 * 1024 * 1024),
    )


def local(
    start_guess,
    right_side,
    root_diagonal,
    preconditioner,
    border_block,
    coupling_inverse,
    border_count,
    column_tiles,
):
    rows, cols = start_guess.shape
    shape = jax.ShapeDtypeStruct
    where = jnp.stack(
        [*(lax.axis_index(a).astype(jnp.int32) for a in (Y, X, Z, CORE, SIDE)), border_count[0]]
    )
    border, inverse = border_block[0], coupling_inverse[0]
    tiles = column_tiles.shape[1]
    everywhere = RING * RING * RING

    line = line_gather(start_guess.astype(BF16))
    span = preconditioner.shape[1] // RING

    def for_ahead(k):
        first = ((where[0] + k) % RING) * span
        return lax.dynamic_slice_in_dim(preconditioner, first, span, 1)

    block1 = to_ahead(for_ahead(1), Y, 1)
    other_tiles = swap(column_tiles, CORE)
    line, block1, other_tiles, border_late, inverse_late, right_side = lax.optimization_barrier(
        (line, block1, other_tiles, border, inverse, right_side)
    )
    border_other = swap(border_late, SIDE)
    inverse_other = swap(inverse_late, SIDE)
    plane = jnp.concatenate([line] + [across(line, -k, 1) for k in range(1, RING)])
    gathered = [plane] + [across(plane, -k, 0) for k in range(1, RING)]

    own_half, for_other = call(
        pick_kernel,
        [SMEM] * 3 + [VMEM] * 4,
        [shape((tiles, HALF, cols), BF16)] * 2,
    )(where, column_tiles, other_tiles, *gathered)
    other_half = swap(for_other, CORE)
    keep, send = call(
        scenario_kernel,
        [SMEM] + [VMEM] * 6,
        [shape((tiles, HALF, cols), F32)] * 2,
        [pltpu.VMEM((tiles * TILE, cols), BF16), pltpu.VMEM((2 * border.shape[0], cols), BF16)],
    )(where, own_half, other_half, border, border_other, inverse, inverse_other)
    arrived = swap(send, CORE)
    near_tiles = RING * RING
    near_shape = (near_tiles, HALF, cols)
    near, *chunks = call(
        scatter_kernel,
        [SMEM] * 3 + [VMEM] * 2,
        [shape(near_shape, F32)] + [shape(near_shape, BF16)] * (RING - 1),
        [pltpu.VMEM((everywhere, HALF, cols), F32)],
    )(where, column_tiles, other_tiles, keep, arrived)
    plane = near
    for k, chunk in enumerate(chunks):
        plane = plane + across(chunk, k + 1, 0).astype(F32)
    plane = plane.reshape(RING, RING, HALF, cols)
    line = plane[0]
    for k in range(1, RING):
        line = line + across(plane[k].astype(BF16), k, 1).astype(F32)
    columns2, columns3, line = lax.optimization_barrier((for_ahead(2), for_ahead(3), line))
    block2, block3 = to_ahead(columns2, Y, 2), to_ahead(columns3, Y, 3)
    own_terms = right_side - root_diagonal[:, None] * start_guess
    line = line + jnp.concatenate([own_terms[None], jnp.zeros_like(line[1:])])
    met = pair(Z, line.astype(BF16), True).astype(F32)
    line = line + jnp.stack([met[1], met[0], met[3], met[2]])
    met = pair(Z, line.astype(BF16), False).astype(F32)
    line = line + jnp.concatenate([met[2:], met[:2]])

    mine = ring_pieces(line.astype(BF16), X)
    mine[0], mine[1] = lax.optimization_barrier((mine[0], mine[1]))
    partners = [swap(piece, CORE) for piece in mine]
    parts = call(
        update_kernel,
        [SMEM] + [VMEM] * 13,
        [shape((rows, cols), F32)] * RING,
        [pltpu.VMEM((span, cols), BF16)],
    )(where, start_guess, preconditioner, block1, block2, block3, *mine, *partners)
    out = parts[0]
    for k in range(1, RING):
        out = out + from_ahead(parts[k], Y, k)
    return out


def solution(mesh):
    torus = Mesh(
        mesh.devices.reshape(RING, RING, RING, mesh.shape["rootr"], mesh.shape["rootc"]),
        (Y, X, Z, CORE, SIDE),
    )
    in_specs = (
        P(SCEN_ROOTR, SIDE),
        P(SCEN_ROOTR, SIDE),
        P(SCEN_ROOTR),
        P(SCEN_ROOTR, None),
        P(SCEN_ROOTR, SIDE, None),
        P(SCEN_ROOTR, SIDE, None),
        P(SCEN_ROOTR),
        P(SCEN_ROOTR, None),
    )
    return jax.shard_map(
        local, mesh=torus, in_specs=in_specs, out_specs=P(SCEN_ROOTR, SIDE), check_vma=False
    )
```

```python
import functools

import jax
import jax.numpy as jnp
from jax import lax
from jax.experimental import pallas as pl
from jax.experimental.pallas import tpu as pltpu
from jax.sharding import Mesh
from jax.sharding import PartitionSpec as P

TILE = 128
HALF = 64
RING = 4
Y, X, Z, CORE, SIDE = "scen_0", "scen_1", "scen_2", "rootr", "rootc"
SCEN_ROOTR = (Y, X, Z, CORE)
SWAP = [(0, 1), (1, 0)]
F32 = jnp.float32
BF16 = jnp.bfloat16

VMEM = pl.BlockSpec(memory_space=pltpu.VMEM)
SMEM = pl.BlockSpec(memory_space=pltpu.SMEM)


def swap(value, axis):
    return lax.ppermute(value, axis, SWAP)


def from_ahead(value, axis, distance):
    return lax.ppermute(value, axis, [(i, (i - distance) % RING) for i in range(RING)])


def to_ahead(value, axis, distance):
    return lax.ppermute(value, axis, [(i, (i + distance) % RING) for i in range(RING)])


def ring_pieces(value, axis):
    return [value] + [from_ahead(value, axis, k) for k in range(1, RING)]


def across(value, distance, turn):
    pairs = []
    for y in range(RING):
        for x in range(RING):
            for core in range(2):
                if core == turn:
                    there = ((y + distance) % RING, x)
                else:
                    there = (y, (x + distance) % RING)
                pairs.append(((y * RING + x) * 2 + core, (there[0] * RING + there[1]) * 2 + core))
    return lax.ppermute(value, (Y, X, CORE), pairs)


def pair(value, first):
    pairs = []
    for z in range(RING):
        for core in range(2):
            other = z ^ 1 if (core == 0) == first else RING - 1 - z
            pairs.append((z * 2 + core, other * 2 + core))
    return lax.ppermute(value, (Z, CORE), pairs)


def line_gather(value):
    two = jnp.stack([value, pair(value, True)])
    return jnp.concatenate([two, pair(two, False)])


def line_slot(tile_z, z, core):
    near, far = z ^ 1, RING - 1 - z
    near_slot = 1 + core
    return jnp.where(
        tile_z == z, 0, jnp.where(tile_z == near, near_slot, jnp.where(tile_z == far, 3 - near_slot, 3))
    )


def spread_place(tile, where):
    dy = (tile // 16 - where[0] + RING) % RING
    dx = ((tile // RING) % RING - where[1] + RING) % RING
    slot = line_slot(tile % RING, where[2], where[3])
    first = where[3] == 0
    return jnp.where(first, dy, dx), jnp.where(first, dx, dy) * RING + slot


def pick_kernel(where, own_ids, other_ids, p0, p1, p2, p3, own_ref, other_ref):
    for ids, out in ((other_ids, other_ref), (own_ids, own_ref)):
        for j in range(ids.shape[1]):
            chunk, rest = spread_place(ids[0, j], where)
            value = p0[rest]
            for k, piece in enumerate((p1, p2, p3)):
                value = jnp.where(chunk == k + 1, piece[rest], value)
            out[j] = value


def scenario_kernel(
    where, own_picked, other_picked, border_own, border_other, inverse_own, inverse_other,
    keep_ref, send_ref, picked, values,
):
    core, side = where[3], where[4]
    half_rows = border_own.shape[0]
    tiles = own_picked.shape[0]
    for j in range(tiles):
        picked[pl.ds(pl.multiple_of(j * TILE + core * HALF, HALF), HALF), :] = own_picked[j]
        picked[pl.ds(pl.multiple_of(j * TILE + (1 - core) * HALF, HALF), HALF), :] = other_picked[j]
    rows = lax.broadcasted_iota(jnp.int32, (half_rows, values.shape[1]), 0)
    own_start = pl.multiple_of(side * half_rows, half_rows)
    other_start = pl.multiple_of((1 - side) * half_rows, half_rows)
    live = where[5]

    def masked(product, start):
        return jnp.where(rows + start < live, product, 0.0).astype(BF16)

    whole = picked[...]
    values[pl.ds(own_start, half_rows), :] = masked(
        jnp.dot(border_own[...], whole, preferred_element_type=F32), own_start
    )
    values[pl.ds(other_start, half_rows), :] = masked(
        jnp.dot(border_other[...], whole, preferred_element_type=F32), other_start
    )
    operand = values[...]
    solved_own = masked(jnp.dot(inverse_own[...], operand, preferred_element_type=F32), own_start)
    solved_other = masked(jnp.dot(inverse_other[...], operand, preferred_element_type=F32), other_start)
    numbers = (((0,), (0,)), ((), ()))
    term = lax.dot_general(border_own[...], solved_own, numbers, preferred_element_type=F32)
    term += lax.dot_general(border_other[...], solved_other, numbers, preferred_element_type=F32)
    term = term.reshape(tiles, 2, HALF, term.shape[1])

    @pl.when(core == 0)
    def _():
        keep_ref[...] = term[:, 0]
        send_ref[...] = term[:, 1]

    @pl.when(core == 1)
    def _():
        keep_ref[...] = term[:, 1]
        send_ref[...] = term[:, 0]


def scatter_kernel(where, own_ids, other_ids, keep, arrived, near, c1, c2, c3, total):
    spots = []
    for ids in (own_ids, other_ids):
        for j in range(ids.shape[1]):
            chunk, rest = spread_place(ids[0, j], where)
            spots.append((chunk, rest, chunk * 16 + rest))
    half = len(spots) // 2
    outs = (near, c1, c2, c3)
    for out in outs:
        out[...] = jnp.zeros_like(out)
    for _, _, spot in spots[half:]:
        total[spot] = jnp.zeros_like(total[spot])
    for j, (_, _, spot) in enumerate(spots[:half]):
        total[spot] = keep[j]
    for j, (_, _, spot) in enumerate(spots[half:]):
        total[spot] += arrived[j]
    for chunk, rest, spot in spots:
        value = total[spot]
        for k, out in enumerate(outs):
            out[rest] = jnp.where(chunk == k, value.astype(out.dtype), out[rest])


def update_kernel(where, start, precond, b1, b2, b3, *refs):
    pieces, (o0, o1, o2, o3, whole) = refs[:8], refs[8:]
    y, x, z, core = where[0], where[1], where[2], where[3]
    near, far = z ^ 1, RING - 1 - z
    for side in range(2):
        half = core if side == 0 else 1 - core
        slots = (z, jnp.where(half == 0, near, far), jnp.where(half == 0, far, near), far ^ 1)
        for i in range(RING):
            piece = pieces[side * RING + i]
            base = ((x + i) % RING) * 4
            for j in range(RING):
                at = pl.multiple_of((base + slots[j]) * TILE + half * HALF, HALF)
                whole[pl.ds(at, HALF), :] = piece[j]
    operand = whole[...]
    span = operand.shape[0]
    own = precond[:, pl.ds(pl.multiple_of(y * span, span), span)]
    o0[...] = start[...] + jnp.dot(own, operand, preferred_element_type=F32)
    for block, out in ((b1, o1), (b2, o2), (b3, o3)):
        out[...] = jnp.dot(block[...], operand, preferred_element_type=F32)


def call(kernel, specs, outs, scratch=(), flops=0, moved=0):
    return pl.pallas_call(
        kernel,
        out_shape=outs,
        in_specs=specs,
        out_specs=jax.tree.map(lambda _: VMEM, outs),
        scratch_shapes=scratch,
        cost_estimate=pl.CostEstimate(flops=flops, bytes_accessed=moved, transcendentals=0),
        compiler_params=pltpu.CompilerParams(vmem_limit_bytes=32 * 1024 * 1024),
    )


def local(
    start_guess,
    right_side,
    root_diagonal,
    preconditioner,
    border_block,
    coupling_inverse,
    border_count,
    column_tiles,
):
    rows, cols = start_guess.shape
    shape = jax.ShapeDtypeStruct
    where = jnp.stack(
        [*(lax.axis_index(a).astype(jnp.int32) for a in (Y, X, Z, CORE, SIDE)), border_count[0]]
    )
    border, inverse = border_block[0], coupling_inverse[0]
    tiles = column_tiles.shape[1]
    everywhere = RING * RING * RING

    line = line_gather(start_guess.astype(BF16))
    span = preconditioner.shape[1] // RING

    def for_ahead(k):
        first = ((where[0] + k) % RING) * span
        return lax.dynamic_slice_in_dim(preconditioner, first, span, 1)

    block1 = to_ahead(for_ahead(1), Y, 1)
    other_tiles = swap(column_tiles, CORE)
    line, block1, other_tiles, border_late, inverse_late, right_side = lax.optimization_barrier(
        (line, block1, other_tiles, border, inverse, right_side)
    )
    border_other = swap(border_late, SIDE)
    inverse_other = swap(inverse_late, SIDE)
    plane = jnp.concatenate([line] + [across(line, -k, 1) for k in range(1, RING)])
    gathered = [plane] + [across(plane, -k, 0) for k in range(1, RING)]

    own_half, for_other = call(
        pick_kernel,
        [SMEM] * 3 + [VMEM] * 4,
        [shape((tiles, HALF, cols), BF16)] * 2,
    )(where, column_tiles, other_tiles, *gathered)
    other_half = swap(for_other, CORE)
    keep, send = call(
        scenario_kernel,
        [SMEM] + [VMEM] * 6,
        [shape((tiles, HALF, cols), F32)] * 2,
        [pltpu.VMEM((tiles * TILE, cols), BF16), pltpu.VMEM((2 * border.shape[0], cols), BF16)],
    )(where, own_half, other_half, border, border_other, inverse, inverse_other)
    arrived = swap(send, CORE)
    near_tiles = RING * RING
    near_shape = (near_tiles, HALF, cols)
    near, *chunks = call(
        scatter_kernel,
        [SMEM] * 3 + [VMEM] * 2,
        [shape(near_shape, F32)] + [shape(near_shape, BF16)] * (RING - 1),
        [pltpu.VMEM((everywhere, HALF, cols), F32)],
    )(where, column_tiles, other_tiles, keep, arrived)
    plane = near
    for k, chunk in enumerate(chunks):
        plane = plane + across(chunk, k + 1, 0).astype(F32)
    plane = plane.reshape(RING, RING, HALF, cols)
    line = plane[0]
    for k in range(1, RING):
        line = line + across(plane[k].astype(BF16), k, 1).astype(F32)
    columns2, columns3, line = lax.optimization_barrier((for_ahead(2), for_ahead(3), line))
    block2, block3 = to_ahead(columns2, Y, 2), to_ahead(columns3, Y, 3)
    own_terms = right_side - root_diagonal[:, None] * start_guess
    line = line + jnp.concatenate([own_terms[None], jnp.zeros_like(line[1:])])
    met = pair(line.astype(BF16), True).astype(F32)
    line = line + jnp.stack([met[1], met[0], met[3], met[2]])
    met = pair(line.astype(BF16), False).astype(F32)
    line = line + jnp.concatenate([met[2:], met[:2]])

    mine = ring_pieces(line.astype(BF16), X)
    mine[0], mine[1] = lax.optimization_barrier((mine[0], mine[1]))
    partners = [swap(piece, CORE) for piece in mine]
    parts = call(
        update_kernel,
        [SMEM] + [VMEM] * 13,
        [shape((rows, cols), F32)] * RING,
        [pltpu.VMEM((span, cols), BF16)],
    )(where, start_guess, preconditioner, block1, block2, block3, *mine, *partners)
    out = parts[0]
    for k in range(1, RING):
        out = out + from_ahead(parts[k], Y, k)
    return out


def solution(mesh):
    torus = Mesh(
        mesh.devices.reshape(RING, RING, RING, mesh.shape["rootr"], mesh.shape["rootc"]),
        (Y, X, Z, CORE, SIDE),
    )
    in_specs = (
        P(SCEN_ROOTR, SIDE),
        P(SCEN_ROOTR, SIDE),
        P(SCEN_ROOTR),
        P(SCEN_ROOTR, None),
        P(SCEN_ROOTR, SIDE, None),
        P(SCEN_ROOTR, SIDE, None),
        P(SCEN_ROOTR),
        P(SCEN_ROOTR, None),
    )
    return jax.shard_map(
        local, mesh=torus, in_specs=in_specs, out_specs=P(SCEN_ROOTR, SIDE), check_vma=False
    )
```

```python
import functools

import jax
import jax.numpy as jnp
from jax import lax
from jax.experimental import pallas as pl
from jax.experimental.pallas import tpu as pltpu
from jax.sharding import Mesh
from jax.sharding import PartitionSpec as P

TILE = 128
HALF = 64
RING = 4
Y, X, Z, CORE, SIDE = "scen_0", "scen_1", "scen_2", "rootr", "rootc"
SCEN_ROOTR = (Y, X, Z, CORE)
SWAP = [(0, 1), (1, 0)]
F32 = jnp.float32
BF16 = jnp.bfloat16

VMEM = pl.BlockSpec(memory_space=pltpu.VMEM)
SMEM = pl.BlockSpec(memory_space=pltpu.SMEM)


def swap(value, axis):
    return lax.ppermute(value, axis, SWAP)


def from_ahead(value, axis, distance):
    return lax.ppermute(value, axis, [(i, (i - distance) % RING) for i in range(RING)])


def to_ahead(value, axis, distance):
    return lax.ppermute(value, axis, [(i, (i + distance) % RING) for i in range(RING)])


def ring_pieces(value, axis):
    return [value] + [from_ahead(value, axis, k) for k in range(1, RING)]


def across(value, distance, turn):
    pairs = []
    for y in range(RING):
        for x in range(RING):
            for core in range(2):
                if core == turn:
                    there = ((y + distance) % RING, x)
                else:
                    there = (y, (x + distance) % RING)
                pairs.append(((y * RING + x) * 2 + core, (there[0] * RING + there[1]) * 2 + core))
    return lax.ppermute(value, (Y, X, CORE), pairs)


def pair(value, first):
    pairs = []
    for z in range(RING):
        for core in range(2):
            other = z ^ 1 if (core == 0) == first else RING - 1 - z
            pairs.append((z * 2 + core, other * 2 + core))
    return lax.ppermute(value, (Z, CORE), pairs)


def line_gather(value):
    two = jnp.stack([value, pair(value, True)])
    return jnp.concatenate([two, pair(two, False)])


def line_slot(tile_z, z, core):
    near, far = z ^ 1, RING - 1 - z
    near_slot = 1 + core
    return jnp.where(
        tile_z == z, 0, jnp.where(tile_z == near, near_slot, jnp.where(tile_z == far, 3 - near_slot, 3))
    )


def spread_place(tile, where):
    dy = (tile // 16 - where[0] + RING) % RING
    dx = ((tile // RING) % RING - where[1] + RING) % RING
    slot = line_slot(tile % RING, where[2], where[3])
    first = where[3] == 0
    return jnp.where(first, dy, dx), jnp.where(first, dx, dy) * RING + slot


def pick_kernel(where, own_ids, other_ids, p0, p1, p2, p3, own_ref, other_ref):
    for ids, out in ((other_ids, other_ref), (own_ids, own_ref)):
        for j in range(ids.shape[1]):
            chunk, rest = spread_place(ids[0, j], where)
            value = p0[rest]
            for k, piece in enumerate((p1, p2, p3)):
                value = jnp.where(chunk == k + 1, piece[rest], value)
            out[j] = value


def scenario_kernel(
    where, own_picked, other_picked, border_own, border_other, inverse_own, inverse_other,
    keep_ref, send_ref, picked, values,
):
    core, side = where[3], where[4]
    half_rows = border_own.shape[0]
    tiles = own_picked.shape[0]
    for j in range(tiles):
        picked[pl.ds(pl.multiple_of(j * TILE + core * HALF, HALF), HALF), :] = own_picked[j]
        picked[pl.ds(pl.multiple_of(j * TILE + (1 - core) * HALF, HALF), HALF), :] = other_picked[j]
    rows = lax.broadcasted_iota(jnp.int32, (half_rows, values.shape[1]), 0)
    own_start = pl.multiple_of(side * half_rows, half_rows)
    other_start = pl.multiple_of((1 - side) * half_rows, half_rows)
    live = where[5]

    def masked(product, start):
        return jnp.where(rows + start < live, product, 0.0).astype(BF16)

    whole = picked[...]
    values[pl.ds(own_start, half_rows), :] = masked(
        jnp.dot(border_own[...], whole, preferred_element_type=F32), own_start
    )
    values[pl.ds(other_start, half_rows), :] = masked(
        jnp.dot(border_other[...], whole, preferred_element_type=F32), other_start
    )
    operand = values[...]
    solved_own = masked(jnp.dot(inverse_own[...], operand, preferred_element_type=F32), own_start)
    solved_other = masked(jnp.dot(inverse_other[...], operand, preferred_element_type=F32), other_start)
    numbers = (((0,), (0,)), ((), ()))
    term = lax.dot_general(border_own[...], solved_own, numbers, preferred_element_type=F32)
    term += lax.dot_general(border_other[...], solved_other, numbers, preferred_element_type=F32)
    term = term.reshape(tiles, 2, HALF, term.shape[1])

    @pl.when(core == 0)
    def _():
        keep_ref[...] = term[:, 0]
        send_ref[...] = term[:, 1]

    @pl.when(core == 1)
    def _():
        keep_ref[...] = term[:, 1]
        send_ref[...] = term[:, 0]


def scatter_kernel(where, own_ids, other_ids, keep, arrived, near, c1, c2, c3, total):
    spots = []
    for ids in (own_ids, other_ids):
        for j in range(ids.shape[1]):
            chunk, rest = spread_place(ids[0, j], where)
            spots.append((chunk, rest, chunk * 16 + rest))
    half = len(spots) // 2
    outs = (near, c1, c2, c3)
    for out in outs:
        out[...] = jnp.zeros_like(out)
    for _, _, spot in spots[half:]:
        total[spot] = jnp.zeros_like(total[spot])
    for j, (_, _, spot) in enumerate(spots[:half]):
        total[spot] = keep[j]
    for j, (_, _, spot) in enumerate(spots[half:]):
        total[spot] += arrived[j]
    for chunk, rest, spot in spots:
        value = total[spot]
        for k, out in enumerate(outs):
            out[rest] = jnp.where(chunk == k, value.astype(out.dtype), out[rest])


def update_kernel(where, start, precond, b1, b2, b3, *refs):
    mine, (early, late), (o0, o1, o2, o3, whole) = refs[:4], refs[4:6], refs[6:]
    swapped = (early, 0), (late, 0), (late, RING), (early, RING)
    y, x, z, core = where[0], where[1], where[2], where[3]
    near, far = z ^ 1, RING - 1 - z
    for side in range(2):
        half = core if side == 0 else 1 - core
        slots = (z, jnp.where(half == 0, near, far), jnp.where(half == 0, far, near), far ^ 1)
        for i in range(RING):
            piece, skip = (mine[i], 0) if side == 0 else swapped[i]
            base = ((x + i) % RING) * 4
            for j in range(RING):
                at = pl.multiple_of((base + slots[j]) * TILE + half * HALF, HALF)
                whole[pl.ds(at, HALF), :] = piece[skip + j]
    operand = whole[...]
    span = operand.shape[0]
    own = precond[:, pl.ds(pl.multiple_of(y * span, span), span)]
    o0[...] = start[...] + jnp.dot(own, operand, preferred_element_type=F32)
    for block, out in ((b1, o1), (b2, o2), (b3, o3)):
        out[...] = jnp.dot(block[...], operand, preferred_element_type=F32)


def call(kernel, specs, outs, scratch=(), flops=0, moved=0):
    return pl.pallas_call(
        kernel,
        out_shape=outs,
        in_specs=specs,
        out_specs=jax.tree.map(lambda _: VMEM, outs),
        scratch_shapes=scratch,
        cost_estimate=pl.CostEstimate(flops=flops, bytes_accessed=moved, transcendentals=0),
        compiler_params=pltpu.CompilerParams(vmem_limit_bytes=32 * 1024 * 1024),
    )


def local(
    start_guess,
    right_side,
    root_diagonal,
    preconditioner,
    border_block,
    coupling_inverse,
    border_count,
    column_tiles,
):
    rows, cols = start_guess.shape
    shape = jax.ShapeDtypeStruct
    where = jnp.stack(
        [*(lax.axis_index(a).astype(jnp.int32) for a in (Y, X, Z, CORE, SIDE)), border_count[0]]
    )
    border, inverse = border_block[0], coupling_inverse[0]
    tiles = column_tiles.shape[1]
    everywhere = RING * RING * RING

    line = line_gather(start_guess.astype(BF16))
    span = preconditioner.shape[1] // RING

    def for_ahead(k):
        first = ((where[0] + k) % RING) * span
        return lax.dynamic_slice_in_dim(preconditioner, first, span, 1)

    block1 = to_ahead(for_ahead(1), Y, 1)
    other_tiles = swap(column_tiles, CORE)
    line, block1, other_tiles, border_late, inverse_late, right_side = lax.optimization_barrier(
        (line, block1, other_tiles, border, inverse, right_side)
    )
    border_other = swap(border_late, SIDE)
    inverse_other = swap(inverse_late, SIDE)
    plane = jnp.concatenate([line] + [across(line, -k, 1) for k in range(1, RING)])
    gathered = [plane] + [across(plane, -k, 0) for k in range(1, RING)]

    own_half, for_other = call(
        pick_kernel,
        [SMEM] * 3 + [VMEM] * 4,
        [shape((tiles, HALF, cols), BF16)] * 2,
    )(where, column_tiles, other_tiles, *gathered)
    other_half = swap(for_other, CORE)
    keep, send = call(
        scenario_kernel,
        [SMEM] + [VMEM] * 6,
        [shape((tiles, HALF, cols), F32)] * 2,
        [pltpu.VMEM((tiles * TILE, cols), BF16), pltpu.VMEM((2 * border.shape[0], cols), BF16)],
    )(where, own_half, other_half, border, border_other, inverse, inverse_other)
    arrived = swap(send, CORE)
    near_tiles = RING * RING
    near_shape = (near_tiles, HALF, cols)
    near, *chunks = call(
        scatter_kernel,
        [SMEM] * 3 + [VMEM] * 2,
        [shape(near_shape, F32)] + [shape(near_shape, BF16)] * (RING - 1),
        [pltpu.VMEM((everywhere, HALF, cols), F32)],
    )(where, column_tiles, other_tiles, keep, arrived)
    plane = near
    for k, chunk in enumerate(chunks):
        plane = plane + across(chunk, k + 1, 0).astype(F32)
    plane = plane.reshape(RING, RING, HALF, cols)
    line = plane[0]
    for k in range(1, RING):
        line = line + across(plane[k].astype(BF16), k, 1).astype(F32)
    columns2, columns3, line = lax.optimization_barrier((for_ahead(2), for_ahead(3), line))
    block2, block3 = to_ahead(columns2, Y, 2), to_ahead(columns3, Y, 3)
    own_terms = right_side - root_diagonal[:, None] * start_guess
    line = line + jnp.concatenate([own_terms[None], jnp.zeros_like(line[1:])])
    met = pair(line.astype(BF16), True).astype(F32)
    line = line + jnp.stack([met[1], met[0], met[3], met[2]])
    met = pair(line.astype(BF16), False).astype(F32)
    line = line + jnp.concatenate([met[2:], met[:2]])

    mine = ring_pieces(line.astype(BF16), X)
    mine[1], mine[2], block2, block3 = lax.optimization_barrier((mine[1], mine[2], block2, block3))
    partners = [
        swap(jnp.concatenate([mine[0], mine[3]]), CORE),
        swap(jnp.concatenate([mine[1], mine[2]]), CORE),
    ]
    parts = call(
        update_kernel,
        [SMEM] + [VMEM] * 11,
        [shape((rows, cols), F32)] * RING,
        [pltpu.VMEM((span, cols), BF16)],
    )(where, start_guess, preconditioner, block1, block2, block3, *mine, *partners)
    out = parts[0]
    for k in range(1, RING):
        out = out + from_ahead(parts[k], Y, k)
    return out


def solution(mesh):
    torus = Mesh(
        mesh.devices.reshape(RING, RING, RING, mesh.shape["rootr"], mesh.shape["rootc"]),
        (Y, X, Z, CORE, SIDE),
    )
    in_specs = (
        P(SCEN_ROOTR, SIDE),
        P(SCEN_ROOTR, SIDE),
        P(SCEN_ROOTR),
        P(SCEN_ROOTR, None),
        P(SCEN_ROOTR, SIDE, None),
        P(SCEN_ROOTR, SIDE, None),
        P(SCEN_ROOTR),
        P(SCEN_ROOTR, None),
    )
    return jax.shard_map(
        local, mesh=torus, in_specs=in_specs, out_specs=P(SCEN_ROOTR, SIDE), check_vma=False
    )
```
